128 devices in a mesh: section: 8 (over z, x_lo), tp: 16 (over y, x_hi, core).
Axes of the slice: x: 4 (x_hi: 2, x_lo: 2; x = x_hi * 2 + x_lo), y: 4, z: 4, core: 2. Of those that a mesh axis runs over, the one named last changes fastest.
Arguments:
- teacher_rows: bfloat16 [8, 256, 8192], P('section', 'tp'), may hold values from -72 to 72
- norm_gain: float32 [8, 8192], P('section'), may hold values from 0.1 to 1.9
- query_weight: bfloat16 [8, 8192, 8192], P('section', None, 'tp'), may hold values from -2.762136 to 2.762136
- keys_values: bfloat16 [8, 2, 8192, 1024], P('section', None, None, 'tp'), may hold values from -0.071815532 to 0.071815532
- output_weight: bfloat16 [8, 8192, 8192], P('section', 'tp'), may hold values from -0.5 to 0.5
- doc_start: int32 [8], P('section'), may hold values from 1 to 255
- student_rows: bfloat16 [8, 256, 4096], P('section', 'tp'), may hold values from -30 to 30
- projector: bfloat16 [4096, 8192], P('tp', 'section'), may hold values from -1 to 2
Outputs:
- teacher_next: bfloat16 [8, 256, 8192], P('section', 'tp')
- distill_loss: float32 [], replicated
- grad_student: float32 [8, 256, 4096], P('section', 'tp')
- grad_projector: float32 [4096, 8192], P('tp', 'section')
The draws below stay inside these ranges and needn't reach their ends.
All inputs are finite; a program needn't handle non-finite values.
Results may differ from the reference program's by a relative error of at most 0.02.
Values may be sent and summed in bfloat16 or wider, within the bound.
No kernel may reach another device: no remote copies, remote signals or barrier semaphores. Data moves between devices by JAX's collectives and lax.ppermute only.
A program may use at most 128 MiB of HBM per device.

```python
import math
import jax
import jax.numpy as jnp
from jax import lax

DT = 8192
DS = 4096
QH = 64
KVH = 8
HD = 128
TROWS = 256
N_SECTION = 8
N_TP = 16


def common_keys(key):
    raw = jax.random.normal(jax.random.fold_in(key, 101), (N_SECTION, 2, DT, KVH * HD), jnp.float32)
    return jnp.clip(raw, -6.0, 6.0) * (1.0 / math.sqrt(DT))


def draw_keys_values(key, part):
    return common_keys(key).astype(jnp.bfloat16)


def draw_query_weight(key, part):
    base = jax.random.normal(jax.random.fold_in(key, 102), (N_SECTION, DT, QH * HD), jnp.float32)
    base = jnp.clip(base, -6.0, 6.0) * (1.0 / math.sqrt(DT))
    return base.astype(jnp.bfloat16)


def student_parts(key):
    shape = (N_SECTION, TROWS, DS)
    row_scale = jnp.exp(jax.random.uniform(jax.random.fold_in(key, 11), (N_SECTION, TROWS, 1), jnp.float32, minval=-1.15, maxval=1.15))
    col_scale = jnp.exp(jax.random.uniform(jax.random.fold_in(key, 12), (1, 1, DS), jnp.float32, minval=-0.35, maxval=0.35))
    noise = jnp.clip(jax.random.normal(jax.random.fold_in(key, 13), shape, jnp.float32), -6.0, 6.0)
    return (noise * col_scale, row_scale)


def draw_student_rows(key, part):
    unit_rows, row_scale = student_parts(key)
    return (unit_rows * row_scale).astype(jnp.bfloat16)


def draw_teacher_rows(key, part):
    shape = (N_SECTION, TROWS, DT)
    unit_rows, student_scale = student_parts(key)
    column_source = jnp.arange(DT, dtype=jnp.int32) % DS
    aligned = jnp.take(unit_rows, column_source, axis=2)
    row_fraction = (jnp.arange(TROWS, dtype=jnp.int32).astype(jnp.float32) / TROWS).reshape(1, TROWS, 1)
    section_fraction = (jnp.arange(N_SECTION, dtype=jnp.int32).astype(jnp.float32) / N_SECTION).reshape(N_SECTION, 1, 1)
    jitter = jax.random.uniform(jax.random.fold_in(key, 5), (N_SECTION, TROWS, 1), jnp.float32, minval=-0.2, maxval=0.2)
    amount = 1.6 - 1.2 * row_fraction - 1.2 * section_fraction + jitter
    row_scale = jnp.exp(jax.random.uniform(jax.random.fold_in(key, 1), (N_SECTION, TROWS, 1), jnp.float32, minval=-1.15, maxval=1.15))
    col_scale = jnp.exp(jax.random.uniform(jax.random.fold_in(key, 2), (1, 1, DT), jnp.float32, minval=-0.35, maxval=0.35))
    noise = jnp.clip(jax.random.normal(jax.random.fold_in(key, 3), shape, jnp.float32), -6.0, 6.0)
    return ((amount * aligned + 0.5 * noise) * row_scale * col_scale).astype(jnp.bfloat16)


def draw_projector(key, part):
    rows_index = jnp.arange(DS, dtype=jnp.int32)
    cols_index = jnp.arange(DT, dtype=jnp.int32) % DS
    tiled = (rows_index[:, None] == cols_index[None, :]).astype(jnp.float32)
    noise = jnp.clip(jax.random.normal(jax.random.fold_in(key, 21), (DS, DT), jnp.float32), -6.0, 6.0)
    return (tiled + noise * (0.5 / math.sqrt(DS))).astype(jnp.bfloat16)


def touch_ends(values, own_key, least, largest):
    extent = values.shape
    index_at = [jax.random.randint(jax.random.fold_in(own_key, axis), (), 0, extent[axis]) for axis in range(len(extent))]
    values = values.at[tuple(index_at)].set(least)
    longest = extent.index(max(extent))
    index_at[longest] = (index_at[longest] + 1) % extent[longest]
    return values.at[tuple(index_at)].set(largest)


def shard_levels(stream_key, shape, cuts, low, top_value):
    gain = 1.0
    for position, parts in cuts:
        heights = jax.random.uniform(jax.random.fold_in(jax.random.fold_in(stream_key, 6), position), (parts,), jnp.float32, low / len(cuts), top_value / len(cuts))
        gain = gain * jnp.repeat(jnp.exp(heights), shape[position] // parts).reshape((-1,) + (1,) * (len(shape) - 1 - position))
    return gain


def scatter_about(own_key, shape, scale, most, split=(), held_as=jnp.bfloat16):
    values = jax.random.normal(own_key, shape, jnp.float32) * scale
    if len(split) > 0:
        values = shard_levels(own_key, shape, split, -0.22, 0.18) * values
    return jnp.clip(values, min=-most, max=most).astype(held_as)


def setup_inputs(seed: int = 0) -> dict:
    key_list = jax.random.split(jax.random.key(seed), 9)
    teacher_rows = draw_teacher_rows(jax.random.fold_in(key_list[8], 71), 0)
    norm_gain = jnp.clip(1.0 + 0.18 * jax.random.normal(key_list[1], (N_SECTION, DT), jnp.float32), 0.1, 1.9)
    query_weight = draw_query_weight(jax.random.fold_in(key_list[8], 71), 0)
    keys_values = draw_keys_values(jax.random.fold_in(key_list[8], 71), 0)
    output_weight = scatter_about(key_list[4], (N_SECTION, QH * HD, DT), HD ** -0.5, 0.5, ((0, 8), (1, 16)))
    doc_start = touch_ends(jax.random.randint(key_list[5], (N_SECTION,), 1, TROWS), jax.random.fold_in(key_list[5], 1), 1, TROWS - 1).astype(jnp.int32)
    student_rows = draw_student_rows(jax.random.fold_in(key_list[8], 71), 0)
    projector = draw_projector(jax.random.fold_in(key_list[8], 71), 0)
    return {"teacher_rows": teacher_rows, "norm_gain": norm_gain, "query_weight": query_weight, "keys_values": keys_values, "output_weight": output_weight, "doc_start": doc_start, "student_rows": student_rows, "projector": projector}


LOSS_WEIGHT = 64.0
NORM_EPS = 1e-05
COS_EPS = 1e-06

def round_bf16(values):
    return lax.optimization_barrier(values.astype(jnp.bfloat16)).astype(jnp.float32)

def teacher_layer(span_rows, gain_row, query_mat, key_mat, value_mat, out_mat, first_new):
    rows_float = span_rows.astype(jnp.float32)
    mean_square = lax.optimization_barrier(jnp.mean(rows_float * rows_float, axis=1, keepdims=True))
    normed = (rows_float * lax.rsqrt(mean_square + NORM_EPS) * gain_row[None, :]).astype(jnp.bfloat16)
    queries = jnp.dot(normed, query_mat, preferred_element_type=jnp.float32).astype(jnp.bfloat16)
    keys_all = jnp.dot(normed, key_mat, preferred_element_type=jnp.float32).astype(jnp.bfloat16)
    values_all = jnp.dot(normed, value_mat, preferred_element_type=jnp.float32).astype(jnp.bfloat16)
    row_total = span_rows.shape[0]
    group = QH // KVH
    query_heads = queries.astype(jnp.float32).reshape(row_total, KVH, group, HD)
    key_heads = keys_all.astype(jnp.float32).reshape(row_total, KVH, HD)
    value_heads = values_all.astype(jnp.float32).reshape(row_total, KVH, HD)
    scale = 1.0 / math.sqrt(HD)
    scores = jnp.einsum('qegd,ked->egqk', query_heads, key_heads) * scale
    positions = jnp.arange(row_total, dtype=jnp.int32)
    after_start = positions >= first_new
    visible = (positions[None, :] <= positions[:, None]) & (after_start[None, :] == after_start[:, None])
    scores = jnp.where(visible, scores, -1e+30)
    row_max = lax.optimization_barrier(jnp.max(scores, axis=-1, keepdims=True))
    expo = jnp.where(visible, jnp.exp(scores - row_max), 0.0)
    weights = (expo / lax.optimization_barrier(jnp.sum(expo, axis=-1, keepdims=True))).astype(jnp.bfloat16)
    mixed = jnp.einsum('egqk,ked->qegd', weights.astype(jnp.float32), value_heads)
    mixed = mixed.astype(jnp.bfloat16).reshape(row_total, QH * HD)
    group_cols = QH * HD // N_TP
    mixed_groups = jnp.transpose(mixed.reshape(row_total, N_TP, group_cols), (1, 0, 2))
    out_groups = out_mat.reshape(N_TP, group_cols, DT)

    def group_term(operands):
        return jnp.dot(operands[0], operands[1], preferred_element_type=jnp.float32).astype(jnp.bfloat16)
    partials = lax.map(group_term, (mixed_groups, out_groups))
    attn_sum = lax.optimization_barrier(jnp.sum(lax.optimization_barrier(partials).astype(jnp.float32), axis=0))
    return (rows_float + attn_sum).astype(jnp.bfloat16)

def cosine_step(inner, own_sq, target_sq, student_proj, target):
    inv_own = lax.rsqrt(own_sq + COS_EPS)
    inv_target = lax.rsqrt(target_sq + COS_EPS)
    cosine = inner * inv_own * inv_target
    slope = LOSS_WEIGHT * ((inner * inv_target * inv_own * inv_own * inv_own)[:, None] * student_proj - target * (inv_own * inv_target)[:, None])
    return (cosine, slope.astype(jnp.bfloat16))

def reference(teacher_rows, norm_gain, query_weight, keys_values, output_weight, doc_start, student_rows, projector):
    outputs = []
    for section_index in range(N_SECTION):
        outputs.append(teacher_layer(teacher_rows[section_index], norm_gain[section_index], query_weight[section_index], keys_values[section_index, 0], keys_values[section_index, 1], output_weight[section_index], doc_start[section_index]))
    teacher_next = jnp.stack(outputs, axis=0)
    token_count = N_SECTION * TROWS
    token_rows = student_rows.reshape(token_count, DS)
    target = teacher_next.reshape(token_count, DT).astype(jnp.float32)
    student_proj = jnp.dot(token_rows, projector, preferred_element_type=jnp.float32)
    inner = lax.optimization_barrier(jnp.sum(student_proj * target, axis=1))
    own_sq = lax.optimization_barrier(jnp.sum(student_proj * student_proj, axis=1))
    target_sq = lax.optimization_barrier(jnp.sum(target * target, axis=1))
    cosine, slope = cosine_step(inner, own_sq, target_sq, student_proj, target)
    distill_loss = jnp.mean(1.0 - cosine)
    grad_student = jnp.dot(slope, projector.T, preferred_element_type=jnp.float32).reshape(N_SECTION, TROWS, DS)
    grad_projector = jnp.dot(token_rows.T, slope, preferred_element_type=jnp.float32)
    return (teacher_next, distill_loss, grad_student, grad_projector)
```

```python
import functools
import math

import jax
import jax.numpy as jnp
from jax import lax
from jax.experimental import pallas as pl
from jax.experimental.pallas import tpu as pltpu
from jax.sharding import Mesh
from jax.sharding import PartitionSpec as P

HD = 128
LOSS_WEIGHT = 64.0
NORM_EPS = 1e-05
COS_EPS = 1e-06
CARRY = 128
SEC = ("z", "xl")
TP = ("y", "xh", "c")

VM = pl.BlockSpec(memory_space=pltpu.VMEM)
SM = pl.BlockSpec(memory_space=pltpu.SMEM)
FAR = pl.BlockSpec(memory_space=pltpu.HBM)


def exchange(pieces, axes):
    return lax.all_to_all(pieces, axes, split_axis=0, concat_axis=0, tiled=True)


def swap(value, axis, apart=1):
    count = lax.axis_size(axis)
    return lax.ppermute(value, axis, [(i, i ^ apart) for i in range(count)])


def f32(value):
    return value.astype(jnp.float32)


def kernel_params(mib):
    return pltpu.CompilerParams(vmem_limit_bytes=mib * 2**20)


def far(value):
    return pltpu.with_memory_space_constraint(value, pltpu.HBM)


def fetched(sources, targets, sems):
    copies = [
        pltpu.make_async_copy(s, t, sems.at[i]) for i, (s, t) in enumerate(zip(sources, targets))
    ]
    for copy in copies:
        copy.start()
    return copies


def norm_kernel(x_ref, gain_ref, o_ref):
    x = f32(x_ref[...])
    mean_square = jnp.mean(x * x, axis=1, keepdims=True)
    o_ref[...] = (x * lax.rsqrt(mean_square + NORM_EPS) * gain_ref[...]).astype(jnp.bfloat16)


def normalize(x, gain):
    return pl.pallas_call(
        norm_kernel,
        out_shape=jax.ShapeDtypeStruct(x.shape, jnp.bfloat16),
        in_specs=[VM, VM],
        out_specs=VM,
        compiler_params=kernel_params(4),
        cost_estimate=pl.CostEstimate(
            flops=20 * x.size, bytes_accessed=320 * x.size, transcendentals=x.shape[0]
        ),
        name="normalize",
    )(x, gain)


def attention_kernel(n_shards, chunk, sc_ref, *refs):
    shard_refs = refs[:n_shards]
    wq_hbm, kva_hbm, kvb_hbm, o_ref, q_acc, kv_acc, wq_ref, kva_ref, kvb_ref, sems = refs[n_shards:]
    per, depth = shard_refs[0].shape
    rows = n_shards * per
    half = rows // 2
    dh = kva_ref.shape[1]
    steps = depth // chunk

    def fetch(step):
        cut = pl.ds(pl.multiple_of(step * chunk, chunk), chunk)
        return (
            pltpu.make_async_copy(wq_hbm.at[cut, :], wq_ref.at[cut, :], sems.at[0, step]),
            pltpu.make_async_copy(kva_hbm.at[:, :, cut], kva_ref.at[:, :, cut], sems.at[1, step]),
            pltpu.make_async_copy(kvb_hbm.at[:, :, cut], kvb_ref.at[:, :, cut], sems.at[2, step]),
        )

    for step in range(steps):
        for copy in fetch(step):
            copy.start()
    q_acc[...] = jnp.zeros_like(q_acc)
    kv_acc[...] = jnp.zeros_like(kv_acc)

    @pl.loop(0, steps)
    def _(step):
        for copy in fetch(step):
            copy.wait()
        cut = pl.ds(pl.multiple_of(step * chunk, chunk), chunk)
        x = jnp.concatenate([r[:, cut] for r in shard_refs], axis=0)
        wkv = jnp.concatenate(
            [kva_ref[0, :, cut], kvb_ref[0, :, cut], kva_ref[1, :, cut], kvb_ref[1, :, cut]],
            axis=0,
        )
        q_acc[...] += jnp.dot(x, wq_ref[cut, :], preferred_element_type=jnp.float32)
        kv_acc[...] += lax.dot_general(
            x, wkv, (((1,), (1,)), ((), ())), preferred_element_type=jnp.float32
        )

    core, xh, y, first_new = sc_ref[0], sc_ref[1], sc_ref[2], sc_ref[3]
    low = core == 0
    keys = kv_acc[:, :HD]
    values = kv_acc[:, HD:]
    keys = jnp.where(low, keys, pltpu.roll(keys, dh, axis=1)).astype(jnp.bfloat16)
    values = jnp.where(low, values, pltpu.roll(values, dh, axis=1)).astype(jnp.bfloat16)

    def place(shape, dim):
        i = lax.broadcasted_iota(jnp.int32, shape, dim)
        side = jnp.where(i < half, 1 - core, core)
        chip_x = ((i >> 6) & 1) ^ xh
        chip_y = ((i >> 4) & 3) ^ y
        return (chip_y * 4 + chip_x * 2 + side) * per + (i & (per - 1))

    row, col = place((rows, rows), 0), place((rows, rows), 1)
    visible = (col <= row) & ((col >= first_new) == (row >= first_new))
    scale = 1.0 / math.sqrt(HD)
    for h in range(q_acc.shape[1] // HD):
        head = slice(h * HD, (h + 1) * HD)
        q = q_acc[:, head].astype(jnp.bfloat16)
        scores = (
            lax.dot_general(q, keys, (((1,), (1,)), ((), ())), preferred_element_type=jnp.float32)
            * scale
        )
        scores = jnp.where(visible, scores, -1e30)
        top = jnp.max(scores, axis=1, keepdims=True)
        expo = jnp.where(visible, jnp.exp(scores - top), 0.0)
        weights = (expo / jnp.sum(expo, axis=1, keepdims=True)).astype(jnp.bfloat16)
        mixed = jnp.dot(weights, values, preferred_element_type=jnp.float32)
        o_ref[:, head] = mixed.astype(jnp.bfloat16)


def attention(scalars, shards_in, wq, kv_mine, kv_other, chunk=1024):
    per, depth = shards_in[0].shape
    n_shards = len(shards_in)
    rows = per * n_shards
    cols = wq.shape[1]
    dh = kv_mine.shape[1]
    return pl.pallas_call(
        functools.partial(attention_kernel, n_shards, chunk),
        out_shape=jax.ShapeDtypeStruct((rows, cols), jnp.bfloat16),
        in_specs=[SM] + [VM] * n_shards + [FAR] * 3,
        out_specs=VM,
        scratch_shapes=[
            pltpu.VMEM((rows, cols), jnp.float32),
            pltpu.VMEM((rows, 4 * dh), jnp.float32),
            pltpu.VMEM(wq.shape, jnp.bfloat16),
            pltpu.VMEM(kv_mine.shape, jnp.bfloat16),
            pltpu.VMEM(kv_other.shape, jnp.bfloat16),
            pltpu.SemaphoreType.DMA((3, depth // chunk)),
        ],
        compiler_params=kernel_params(20),
        cost_estimate=pl.CostEstimate(
            flops=2 * rows * depth * (cols + 4 * dh),
            bytes_accessed=2 * (rows * depth + depth * (cols + 4 * dh)),
            transcendentals=4 * rows * rows,
        ),
        name="attention",
    )(scalars, *shards_in, far(wq), far(kv_mine), far(kv_other))


def project_kernel(base, chunk, m_ref, w_hbm, other_ref, own_ref, w_ref, sems):
    half, cols = other_ref.shape
    copies = []
    for step in range(cols // chunk):
        copies.append(
            pltpu.make_async_copy(
                w_hbm.at[:, base + step * chunk : base + (step + 1) * chunk],
                w_ref.at[:, step * chunk : (step + 1) * chunk],
                sems.at[step],
            )
        )
        copies[-1].start()
    for step, copy in enumerate(copies):
        copy.wait()
        cut = slice(step * chunk, (step + 1) * chunk)
        y = jnp.dot(m_ref[...], w_ref[:, cut], preferred_element_type=jnp.float32)
        other_ref[:, cut] = y[:half].astype(jnp.bfloat16)
        own_ref[:, cut] = y[half:].astype(jnp.bfloat16)


def project(mixed, w, base, cols, chunk=512):
    rows, depth = mixed.shape
    out = jax.ShapeDtypeStruct((rows // 2, cols), jnp.bfloat16)
    return pl.pallas_call(
        functools.partial(project_kernel, base, chunk),
        out_shape=(out, out),
        in_specs=[VM, FAR],
        out_specs=(VM, VM),
        scratch_shapes=[
            pltpu.VMEM((depth, cols), jnp.bfloat16),
            pltpu.SemaphoreType.DMA((cols // chunk,)),
        ],
        compiler_params=kernel_params(12),
        cost_estimate=pl.CostEstimate(
            flops=2 * rows * depth * cols,
            bytes_accessed=2 * (rows * depth + depth * cols + rows * cols),
            transcendentals=0,
        ),
        name="project",
    )(mixed, far(w))


def add_kernel(n, *refs):
    outs = refs[2 * n :]
    per = outs[0].shape[0]
    width = refs[0].shape[1]
    for i, out in enumerate(outs):
        cut = slice(i * per, (i + 1) * per)
        for j in range(n):
            total = f32(refs[j][cut, :]) + f32(refs[n + j][cut, :])
            out[:, j * width : (j + 1) * width] = total.astype(jnp.bfloat16)


def add_pieces(kept, arrived, count):
    rows, cols = kept[0].shape
    out = jax.ShapeDtypeStruct((rows // count, cols * len(kept)), jnp.bfloat16)
    return pl.pallas_call(
        functools.partial(add_kernel, len(kept)),
        out_shape=(out,) * count,
        in_specs=[VM] * (2 * len(kept)),
        out_specs=(VM,) * count,
        compiler_params=kernel_params(4),
        name="add_pieces",
    )(*kept, *arrived)


def sum_kernel(*refs):
    total = f32(refs[0][...])
    for r in refs[1:-1]:
        total += f32(r[...])
    refs[-1][...] = total.astype(refs[-1].dtype)


def sum_of(arrays, dtype):
    return pl.pallas_call(
        sum_kernel,
        out_shape=jax.ShapeDtypeStruct(arrays[0].shape, dtype),
        in_specs=[VM] * len(arrays),
        out_specs=VM,
        compiler_params=kernel_params(4),
        name="sum_of",
    )(*arrays)


def slope_kernel(*refs):
    parts = refs[:-4]
    x_ref, sp_ref, next_ref, slope_ref = refs[-4:]
    blocks, rows, width = sp_ref.shape
    inner = jnp.zeros((rows, 1), jnp.float32)
    own_sq = jnp.zeros((rows, 1), jnp.float32)
    target_sq = jnp.zeros((rows, 1), jnp.float32)
    for j in range(blocks):
        cols = slice(j * width, (j + 1) * width)
        total = f32(parts[0][:, cols])
        for p in parts[1:]:
            total += f32(p[:, cols])
        new = (f32(x_ref[:, cols]) + total).astype(jnp.bfloat16)
        next_ref[:, cols] = new
        target = f32(new)
        sp = sp_ref[j]
        inner += jnp.sum(sp * target, axis=1, keepdims=True)
        own_sq += jnp.sum(sp * sp, axis=1, keepdims=True)
        target_sq += jnp.sum(target * target, axis=1, keepdims=True)
    inv_own = lax.rsqrt(own_sq + COS_EPS)
    inv_target = lax.rsqrt(target_sq + COS_EPS)
    cosine = inner * inv_own * inv_target
    toward = inner * inv_target * inv_own * inv_own * inv_own
    away = inv_own * inv_target
    for j in range(blocks):
        cols = slice(j * width, (j + 1) * width)
        slope = LOSS_WEIGHT * (toward * sp_ref[j] - f32(next_ref[:, cols]) * away)
        slope_ref[j, :, :width] = slope.astype(jnp.bfloat16)
    distance = jnp.broadcast_to(1.0 - cosine, (rows, CARRY))
    high = f32(distance.astype(jnp.bfloat16))
    middle = f32((distance - high).astype(jnp.bfloat16))
    low = distance - high - middle
    lane = lax.broadcasted_iota(jnp.int32, (rows, CARRY), 1)
    carried = jnp.where(lane == 0, high, jnp.where(lane == 1, middle, low))
    carried = jnp.where(lane < 3, carried, 0.0).astype(jnp.bfloat16)
    for j in range(blocks):
        slope_ref[j, :, width:] = carried


def slopes(parts, x, sp):
    return pl.pallas_call(
        slope_kernel,
        out_shape=(
            jax.ShapeDtypeStruct(x.shape, jnp.bfloat16),
            jax.ShapeDtypeStruct((*sp.shape[:2], sp.shape[2] + CARRY), jnp.bfloat16),
        ),
        in_specs=[VM] * (len(parts) + 2),
        out_specs=(VM, VM),
        compiler_params=kernel_params(6),
        name="slopes",
    )(*parts, x, sp)


def stacked(refs, all_ref):
    for k, r in enumerate(refs):
        all_ref[:, k] = r[:, :, : all_ref.shape[3]]
    n_sec, n_y, rows, width = all_ref.shape
    return all_ref[...].reshape(n_sec * n_y * rows, width)


def blocks_of(sc_ref, size):
    core, xh = sc_ref[0], sc_ref[1]
    for at_x, at_c in ((xh, core), (xh, 1 - core), (1 - xh, core), (1 - xh, 1 - core)):
        yield pl.ds(pl.multiple_of((at_x * 2 + at_c) * size, size), size)


def student_proj_kernel(n_sends, sc_ref, *refs):
    distant, keep_ref, send_refs = refs[:5], refs[5], refs[6 : 6 + n_sends]
    near, sems = refs[6 + n_sends : -1], refs[-1]
    copies = fetched(distant, near, sems)
    tokens_ref, proj_refs = near[0], near[1:]
    size = proj_refs[0].shape[0]
    total = None
    copies[0].wait()
    for cut, p, copy in zip(blocks_of(sc_ref, size), proj_refs, copies[1:]):
        copy.wait()
        y = jnp.dot(tokens_ref[:, cut], p[...], preferred_element_type=jnp.float32)
        total = y if total is None else total + y
    n_sec, rows, block = keep_ref.shape
    total = total.reshape(n_sec, 1 + n_sends, rows, block)
    keep_ref[...] = total[:, 0]
    for k, out in enumerate(send_refs):
        out[...] = total[:, k + 1].astype(jnp.bfloat16)


def student_proj_part(scalars, tokens, proj, n_sec, n_y):
    n_tok, feats = tokens.shape
    rows, block = n_tok // (n_sec * n_y), proj[0].shape[1]
    keep = jax.ShapeDtypeStruct((n_sec, rows, block), jnp.float32)
    send = jax.ShapeDtypeStruct((n_sec, rows, block), jnp.bfloat16)
    inputs = (tokens, *proj)
    return pl.pallas_call(
        functools.partial(student_proj_kernel, n_y - 1),
        out_shape=(keep,) + (send,) * (n_y - 1),
        in_specs=[SM] + [FAR] * len(inputs),
        out_specs=(VM,) * n_y,
        scratch_shapes=[pltpu.VMEM(v.shape, v.dtype) for v in inputs]
        + [pltpu.SemaphoreType.DMA((len(inputs),))],
        compiler_params=kernel_params(14),
        cost_estimate=pl.CostEstimate(
            flops=2 * n_tok * feats * block,
            bytes_accessed=2 * (n_tok * feats + feats * block + n_tok * block),
            transcendentals=0,
        ),
        name="student_proj_part",
    )(scalars, *map(far, inputs))


def gradients_kernel(n_y, sc_ref, *refs):
    slope_refs, distant = refs[:n_y], refs[n_y : n_y + 5]
    gs_ref, loss_ref, away_far, away_near, stay_far, stay_near = refs[n_y + 5 : n_y + 11]
    all_ref, near, sems = refs[n_y + 11], refs[n_y + 12 : -1], refs[-1]
    copies = fetched(distant, near, sems)
    tokens_ref, proj_refs = near[0], near[1:]
    slope = stacked(slope_refs, all_ref)
    width, size = proj_refs[0].shape
    core, xh = sc_ref[0], sc_ref[1]
    copies[0].wait()
    for out, at_x, at_c in (
        (away_far, 1 - xh, 1 - core),
        (away_near, xh, 1 - core),
        (stay_far, 1 - xh, core),
        (stay_near, xh, core),
    ):
        cut = pl.ds(pl.multiple_of((at_x * 2 + at_c) * size, size), size)
        y = jnp.dot(tokens_ref[cut, :], slope, preferred_element_type=jnp.float32)
        out[...] = y.astype(out.dtype)
    for cut, p, copy in zip(blocks_of(sc_ref, size), proj_refs, copies[1:]):
        copy.wait()
        y = jnp.dot(slope, p[...], preferred_element_type=jnp.float32)
        gs_ref[:, :, :, cut] = y.astype(jnp.bfloat16).reshape(*gs_ref.shape[:3], size)
    loss = None
    for r in slope_refs:
        part = jnp.sum(f32(r[:, :, width:]), axis=(0, 1), keepdims=True)
        loss = part if loss is None else loss + part
    loss = jnp.sum(loss[0], axis=1, keepdims=True)
    loss_ref[...] = jnp.broadcast_to(loss, loss_ref.shape)


def gradients(scalars, slope, tokens_t, proj_t):
    n_y = len(slope)
    n_sec, rows = slope[0].shape[:2]
    width, size = proj_t[0].shape
    low = jax.ShapeDtypeStruct((size, width), jnp.bfloat16)
    high = jax.ShapeDtypeStruct((size, width), jnp.float32)
    inputs = (tokens_t, *proj_t)
    return pl.pallas_call(
        functools.partial(gradients_kernel, n_y),
        out_shape=(
            jax.ShapeDtypeStruct((n_sec, n_y, rows, size * len(proj_t)), jnp.bfloat16),
            jax.ShapeDtypeStruct((8, 128), jnp.float32),
            low,
            low,
            high,
            high,
        ),
        in_specs=[SM] + [VM] * n_y + [FAR] * len(inputs),
        out_specs=(VM,) * 6,
        scratch_shapes=[pltpu.VMEM((n_sec, n_y, rows, width), jnp.bfloat16)]
        + [pltpu.VMEM(v.shape, v.dtype) for v in inputs]
        + [pltpu.SemaphoreType.DMA((len(inputs),))],
        compiler_params=kernel_params(14),
        name="gradients",
    )(scalars, *slope, *map(far, inputs))


def section_sum_kernel(g_ref, *outs):
    for k, out in enumerate(outs):
        total = f32(g_ref[0, k])
        for s in range(1, g_ref.shape[0]):
            total += f32(g_ref[s, k])
        out[...] = total.astype(out.dtype)


def section_sum(g):
    _, n_y, rows, feats = g.shape
    first = jax.ShapeDtypeStruct((rows, feats), jnp.float32)
    rest = jax.ShapeDtypeStruct((rows, feats), jnp.bfloat16)
    return pl.pallas_call(
        section_sum_kernel,
        out_shape=(first,) + (rest,) * (n_y - 1),
        in_specs=[VM],
        out_specs=(VM,) * n_y,
        compiler_params=kernel_params(6),
        name="section_sum",
    )(g)


def place_kernel(sc_ref, *refs):
    o_ref = refs[-1]
    feats = refs[0].shape[1]
    for k, r in enumerate(refs[:-1]):
        cut = pl.ds(pl.multiple_of((sc_ref[2] ^ k) * feats, feats), feats)
        o_ref[:, cut] = f32(r[...])


def placed_feats(scalars, pieces):
    rows, feats = pieces[0].shape
    return pl.pallas_call(
        place_kernel,
        out_shape=jax.ShapeDtypeStruct((rows, feats * len(pieces)), jnp.float32),
        in_specs=[SM] + [VM] * len(pieces),
        out_specs=VM,
        compiler_params=kernel_params(4),
        name="placed_feats",
    )(scalars, *pieces)


def tied(*values):
    return lax.optimization_barrier(values)


def to_columns(value, n_y):
    return [value] + [swap(value, "y", k) for k in range(1, n_y)]


def step(
    teacher_rows,
    norm_gain,
    query_weight,
    keys_values,
    output_weight,
    doc_start,
    student_rows,
    projector,
):
    core = lax.axis_index("c").astype(jnp.int32)
    xh = lax.axis_index("xh").astype(jnp.int32)
    y = lax.axis_index("y").astype(jnp.int32)
    n_sec = lax.axis_size(SEC)
    n_y = lax.axis_size("y")
    n_tp = lax.axis_size(TP)
    x = teacher_rows[0]
    rows, width = x.shape
    scalars = jnp.stack([core, xh, y, doc_start[0]])

    feats = student_rows.shape[2] // n_y
    picked = [
        lax.dynamic_slice_in_dim(student_rows[0], (y ^ k) * feats, feats, axis=1)
        for k in range(n_y)
    ]
    picked = [picked[0]] + [swap(picked[k], "y", k) for k in range(1, n_y)]
    proj = [projector, swap(projector, "c", 1), swap(projector, "xh", 1)]

    normed = normalize(x, norm_gain)
    y1, y3 = swap(normed, "y", 1), swap(normed, "y", 3)
    across = swap(normed, "xh", 1)
    y2 = swap(normed, "y", 2)
    own = [normed, y1, y2, y3]
    own += [across, swap(across, "y", 1), swap(y2, "xh", 1), swap(across, "y", 3)]
    other = [swap(v, "c", 1) for v in own]
    kv_mine = jnp.swapaxes(keys_values[0], 1, 2)
    kv_other = swap(kv_mine, "c", 1)

    mine, _ = tied(jnp.stack(picked), normed)
    tokens = exchange(jnp.broadcast_to(mine, (n_sec, *mine.shape)), SEC)
    n_tok = n_sec * n_y * rows
    tokens = tokens.reshape(n_tok, feats)

    mixed = attention(scalars, other + own, query_weight[0], kv_mine, kv_other)

    proj[2], mixed = tied(proj[2], mixed)
    proj.append(swap(proj[2], "c", 1))
    half = width // 2
    to_other, kept = project(mixed, output_weight[0], 0, half)
    sides = [(kept, to_other, swap(to_other, "c", 1))]

    tokens, _ = tied(tokens, kept)
    keep, *sends = student_proj_part(scalars, tokens, proj, n_sec, n_y)
    mixed, keep = tied(mixed, keep)
    got = [swap(sends[k - 1], "y", k) for k in range(1, n_y)]
    to_other, kept = project(mixed, output_weight[0], half, half)
    sides.append((kept, to_other, swap(to_other, "c", 1)))

    pieces = add_pieces([s[0] for s in sides], [s[2] for s in sides], 2 * n_y)
    near, away = list(pieces[:n_y]), list(pieces[n_y:])
    late = tied(pieces[0], tokens, *proj)
    tokens_t = late[1].T
    proj_t = [p.T for p in late[2:]]
    relayed = swap(away[2], "xh", 1)
    away = sum_of((away[0], swap(away[1], "y", 1), swap(away[3], "y", 3)), jnp.bfloat16)
    away = swap(away, "xh", 1)
    relayed = swap(sum_of((near[2], relayed), jnp.bfloat16), "y", 2)
    parts = (near[0], swap(near[1], "y", 1), swap(near[3], "y", 3), relayed, away)

    sp = sum_of((keep, *got), jnp.float32)
    sp = exchange(sp, SEC)
    sp, tokens_t, *proj_t = tied(sp, tokens_t, *proj_t)
    teacher_next, slope = slopes(parts, x, sp)

    slope = exchange(slope, SEC)
    slope = to_columns(slope, n_y)
    grad_s, loss, away_far, away_near, stay_far, stay_near = gradients(
        scalars, slope, tokens_t, proj_t
    )
    grad_s = exchange(grad_s, SEC)
    loss = loss + swap(loss, "c", 1)
    away_far = swap(away_far, "c", 1)
    away_near = swap(away_near, "c", 1)
    loss = loss + swap(loss, "xh", 1)
    across = swap(sum_of((stay_far, away_far), jnp.bfloat16), "xh", 1)
    grad_projector = sum_of((stay_near, away_near, across), jnp.float32)
    pieces = section_sum(grad_s)
    pieces = [pieces[0]] + [swap(pieces[k], "y", k) for k in range(1, n_y)]
    pieces[3], grad_projector, loss = tied(pieces[3], grad_projector, loss)
    grad_student = placed_feats(scalars, pieces)
    loss = loss[0, 0] / (n_sec * n_tp * rows)
    return (teacher_next[None], loss, grad_student[None], grad_projector)


def solution(mesh):
    fine = Mesh(mesh.devices.reshape(4, 2, 4, 2, 2), ("z", "xl", "y", "xh", "c"))
    placed = (
        P(SEC, TP, None),
        P(SEC, None),
        P(SEC, None, TP),
        P(SEC, None, None, TP),
        P(SEC, TP, None),
        P(SEC),
        P(SEC, TP, None),
        P(TP, SEC),
    )
    return jax.shard_map(
        step,
        mesh=fine,
        in_specs=placed,
        out_specs=(P(SEC, TP, None), P(), P(SEC, TP, None), P(TP, SEC)),
        check_vma=False,
    )
```

```python
import functools
import math

import jax
import jax.numpy as jnp
from jax import lax
from jax.experimental import pallas as pl
from jax.experimental.pallas import tpu as pltpu
from jax.sharding import Mesh
from jax.sharding import PartitionSpec as P

HD = 128
LOSS_WEIGHT = 64.0
NORM_EPS = 1e-05
COS_EPS = 1e-06
CARRY = 128
SEC = ("z", "xl")
TP = ("y", "xh", "c")

VM = pl.BlockSpec(memory_space=pltpu.VMEM)
SM = pl.BlockSpec(memory_space=pltpu.SMEM)
FAR = pl.BlockSpec(memory_space=pltpu.HBM)


def exchange(pieces, axes):
    return lax.all_to_all(pieces, axes, split_axis=0, concat_axis=0, tiled=True)


def swap(value, axis, apart=1):
    count = lax.axis_size(axis)
    return lax.ppermute(value, axis, [(i, i ^ apart) for i in range(count)])


def f32(value):
    return value.astype(jnp.float32)


def kernel_params(mib):
    return pltpu.CompilerParams(vmem_limit_bytes=mib * 2**20)


def far(value):
    return pltpu.with_memory_space_constraint(value, pltpu.HBM)


def fetched(sources, targets, sems):
    copies = [
        pltpu.make_async_copy(s, t, sems.at[i]) for i, (s, t) in enumerate(zip(sources, targets))
    ]
    for copy in copies:
        copy.start()
    return copies


def norm_kernel(x_far, gain_far, o_ref, x_ref, gain_ref, sems):
    for copy in fetched((x_far, gain_far), (x_ref, gain_ref), sems):
        copy.wait()
    x = f32(x_ref[...])
    mean_square = jnp.mean(x * x, axis=1, keepdims=True)
    o_ref[...] = (x * lax.rsqrt(mean_square + NORM_EPS) * gain_ref[...]).astype(jnp.bfloat16)


def normalize(x, gain):
    return pl.pallas_call(
        norm_kernel,
        out_shape=jax.ShapeDtypeStruct(x.shape, jnp.bfloat16),
        in_specs=[FAR, FAR],
        out_specs=VM,
        scratch_shapes=[
            pltpu.VMEM(x.shape, x.dtype),
            pltpu.VMEM(gain.shape, gain.dtype),
            pltpu.SemaphoreType.DMA((2,)),
        ],
        compiler_params=kernel_params(4),
        name="normalize",
    )(far(x), far(gain))


def attention_kernel(n_shards, chunk, sc_ref, *refs):
    n_far = n_shards // 2
    far_refs = refs[:n_far]
    wq_hbm, kva_hbm, kvb_hbm, wo_hbm, o_ref, other_ref, own_ref = refs[n_shards : n_shards + 7]
    q_acc, kv_acc, wq_ref, kva_ref, kvb_ref, wo_ref, held_ref, sems, out_sem, held_sems = refs[
        n_shards + 7 :
    ]
    own_refs = refs[n_far:n_shards]
    per, depth = own_refs[0].shape
    rows = n_shards * per
    half = rows // 2
    dh = kva_ref.shape[1]
    steps = depth // chunk

    def fetch(step):
        cut = pl.ds(pl.multiple_of(step * chunk, chunk), chunk)
        return (
            pltpu.make_async_copy(wq_hbm.at[cut, :], wq_ref.at[cut, :], sems.at[0, step]),
            pltpu.make_async_copy(kva_hbm.at[:, :, cut], kva_ref.at[:, :, cut], sems.at[1, step]),
            pltpu.make_async_copy(kvb_hbm.at[:, :, cut], kvb_ref.at[:, :, cut], sems.at[2, step]),
            *(
                pltpu.make_async_copy(
                    r.at[:, cut], held_ref.at[i * per : (i + 1) * per, cut], held_sems.at[i, step]
                )
                for i, r in enumerate(far_refs)
            ),
        )

    for step in range(steps):
        for copy in fetch(step):
            copy.start()
    half_cols = own_ref.shape[1]
    out_copy = pltpu.make_async_copy(wo_hbm.at[:, :half_cols], wo_ref, out_sem.at[0])
    out_copy.start()
    q_acc[...] = jnp.zeros_like(q_acc)
    kv_acc[...] = jnp.zeros_like(kv_acc)

    @pl.loop(0, steps)
    def _(step):
        for copy in fetch(step):
            copy.wait()
        cut = pl.ds(pl.multiple_of(step * chunk, chunk), chunk)
        x = jnp.concatenate([held_ref[:, cut], *(r[:, cut] for r in own_refs)], axis=0)
        wkv = jnp.concatenate(
            [kva_ref[0, :, cut], kvb_ref[0, :, cut], kva_ref[1, :, cut], kvb_ref[1, :, cut]],
            axis=0,
        )
        q_acc[...] += jnp.dot(x, wq_ref[cut, :], preferred_element_type=jnp.float32)
        kv_acc[...] += lax.dot_general(
            x, wkv, (((1,), (1,)), ((), ())), preferred_element_type=jnp.float32
        )

    core, xh, y, first_new = sc_ref[0], sc_ref[1], sc_ref[2], sc_ref[3]
    low = core == 0
    keys = kv_acc[:, :HD]
    values = kv_acc[:, HD:]
    keys = jnp.where(low, keys, pltpu.roll(keys, dh, axis=1)).astype(jnp.bfloat16)
    values = jnp.where(low, values, pltpu.roll(values, dh, axis=1)).astype(jnp.bfloat16)

    def place(shape, dim):
        i = lax.broadcasted_iota(jnp.int32, shape, dim)
        side = jnp.where(i < half, 1 - core, core)
        chip_x = ((i >> 6) & 1) ^ xh
        chip_y = ((i >> 4) & 3) ^ y
        return (chip_y * 4 + chip_x * 2 + side) * per + (i & (per - 1))

    row, col = place((rows, rows), 0), place((rows, rows), 1)
    visible = (col <= row) & ((col >= first_new) == (row >= first_new))
    scale = 1.0 / math.sqrt(HD)
    for h in range(q_acc.shape[1] // HD):
        head = slice(h * HD, (h + 1) * HD)
        q = q_acc[:, head].astype(jnp.bfloat16)
        scores = (
            lax.dot_general(q, keys, (((1,), (1,)), ((), ())), preferred_element_type=jnp.float32)
            * scale
        )
        scores = jnp.where(visible, scores, -1e30)
        top = jnp.max(scores, axis=1, keepdims=True)
        expo = jnp.where(visible, jnp.exp(scores - top), 0.0)
        weights = (expo / jnp.sum(expo, axis=1, keepdims=True)).astype(jnp.bfloat16)
        mixed = jnp.dot(weights, values, preferred_element_type=jnp.float32)
        o_ref[:, head] = mixed.astype(jnp.bfloat16)
    out_copy.wait()
    for cut in (slice(i, i + 512) for i in range(0, half_cols, 512)):
        y = jnp.dot(o_ref[...], wo_ref[:, cut], preferred_element_type=jnp.float32)
        other_ref[:, cut] = y[:half].astype(jnp.bfloat16)
        own_ref[:, cut] = y[half:].astype(jnp.bfloat16)


def attention(scalars, shards_in, wq, kv_mine, kv_other, wo, chunk=1024):
    per, depth = shards_in[0].shape
    n_shards = len(shards_in)
    rows = per * n_shards
    cols = wq.shape[1]
    dh = kv_mine.shape[1]
    half_cols = wo.shape[1] // 2
    part = jax.ShapeDtypeStruct((rows // 2, half_cols), jnp.bfloat16)
    return pl.pallas_call(
        functools.partial(attention_kernel, n_shards, chunk),
        out_shape=(jax.ShapeDtypeStruct((rows, cols), jnp.bfloat16), part, part),
        in_specs=[SM] + [FAR] * (n_shards // 2) + [VM] * (n_shards // 2) + [FAR] * 4,
        out_specs=(VM,) * 3,
        scratch_shapes=[
            pltpu.VMEM((rows, cols), jnp.float32),
            pltpu.VMEM((rows, 4 * dh), jnp.float32),
            pltpu.VMEM(wq.shape, jnp.bfloat16),
            pltpu.VMEM(kv_mine.shape, jnp.bfloat16),
            pltpu.VMEM(kv_other.shape, jnp.bfloat16),
            pltpu.VMEM((cols, half_cols), jnp.bfloat16),
            pltpu.VMEM((rows // 2, depth), jnp.bfloat16),
            pltpu.SemaphoreType.DMA((3, depth // chunk)),
            pltpu.SemaphoreType.DMA((1,)),
            pltpu.SemaphoreType.DMA((n_shards // 2, depth // chunk)),
        ],
        compiler_params=kernel_params(28),
        cost_estimate=pl.CostEstimate(
            flops=2 * rows * depth * (cols + 4 * dh),
            bytes_accessed=2 * (rows * depth + depth * (cols + 4 * dh)),
            transcendentals=4 * rows * rows,
        ),
        name="attention",
    )(scalars, *map(far, shards_in[: n_shards // 2]), *shards_in[n_shards // 2 :], far(wq), far(kv_mine), far(kv_other), far(wo))


def project_kernel(base, chunk, m_ref, w_hbm, other_ref, own_ref, w_ref, sems):
    half, cols = other_ref.shape
    copies = []
    for step in range(cols // chunk):
        copies.append(
            pltpu.make_async_copy(
                w_hbm.at[:, base + step * chunk : base + (step + 1) * chunk],
                w_ref.at[:, step * chunk : (step + 1) * chunk],
                sems.at[step],
            )
        )
        copies[-1].start()
    for step, copy in enumerate(copies):
        copy.wait()
        cut = slice(step * chunk, (step + 1) * chunk)
        y = jnp.dot(m_ref[...], w_ref[:, cut], preferred_element_type=jnp.float32)
        other_ref[:, cut] = y[:half].astype(jnp.bfloat16)
        own_ref[:, cut] = y[half:].astype(jnp.bfloat16)


def project(mixed, w, base, cols, chunk=512):
    rows, depth = mixed.shape
    out = jax.ShapeDtypeStruct((rows // 2, cols), jnp.bfloat16)
    return pl.pallas_call(
        functools.partial(project_kernel, base, chunk),
        out_shape=(out, out),
        in_specs=[VM, FAR],
        out_specs=(VM, VM),
        scratch_shapes=[
            pltpu.VMEM((depth, cols), jnp.bfloat16),
            pltpu.SemaphoreType.DMA((cols // chunk,)),
        ],
        compiler_params=kernel_params(12),
        cost_estimate=pl.CostEstimate(
            flops=2 * rows * depth * cols,
            bytes_accessed=2 * (rows * depth + depth * cols + rows * cols),
            transcendentals=0,
        ),
        name="project",
    )(mixed, far(w))


def add_kernel(n, *refs):
    outs = refs[2 * n :]
    per = outs[0].shape[0]
    width = refs[0].shape[1]
    for i, out in enumerate(outs):
        cut = slice(i * per, (i + 1) * per)
        for j in range(n):
            total = f32(refs[j][cut, :]) + f32(refs[n + j][cut, :])
            out[:, j * width : (j + 1) * width] = total.astype(jnp.bfloat16)


def add_pieces(kept, arrived, count):
    rows, cols = kept[0].shape
    out = jax.ShapeDtypeStruct((rows // count, cols * len(kept)), jnp.bfloat16)
    return pl.pallas_call(
        functools.partial(add_kernel, len(kept)),
        out_shape=(out,) * count,
        in_specs=[VM] * (2 * len(kept)),
        out_specs=(VM,) * count,
        compiler_params=kernel_params(4),
        name="add_pieces",
    )(*kept, *arrived)


def sum_kernel(*refs):
    total = f32(refs[0][...])
    for r in refs[1:-1]:
        total += f32(r[...])
    refs[-1][...] = total.astype(refs[-1].dtype)


def sum_of(arrays, dtype):
    return pl.pallas_call(
        sum_kernel,
        out_shape=jax.ShapeDtypeStruct(arrays[0].shape, dtype),
        in_specs=[VM] * len(arrays),
        out_specs=VM,
        compiler_params=kernel_params(4),
        name="sum_of",
    )(*arrays)


def slope_kernel(*refs):
    parts = refs[:-4]
    x_ref, sp_ref, next_ref, slope_ref = refs[-4:]
    blocks, rows, width = sp_ref.shape
    inner = jnp.zeros((rows, 1), jnp.float32)
    own_sq = jnp.zeros((rows, 1), jnp.float32)
    target_sq = jnp.zeros((rows, 1), jnp.float32)
    for j in range(blocks):
        cols = slice(j * width, (j + 1) * width)
        total = f32(parts[0][:, cols])
        for p in parts[1:]:
            total += f32(p[:, cols])
        new = (f32(x_ref[:, cols]) + total).astype(jnp.bfloat16)
        next_ref[:, cols] = new
        target = f32(new)
        sp = f32(sp_ref[j])
        inner += jnp.sum(sp * target, axis=1, keepdims=True)
        own_sq += jnp.sum(sp * sp, axis=1, keepdims=True)
        target_sq += jnp.sum(target * target, axis=1, keepdims=True)
    inv_own = lax.rsqrt(own_sq + COS_EPS)
    inv_target = lax.rsqrt(target_sq + COS_EPS)
    cosine = inner * inv_own * inv_target
    toward = inner * inv_target * inv_own * inv_own * inv_own
    away = inv_own * inv_target
    for j in range(blocks):
        cols = slice(j * width, (j + 1) * width)
        slope = LOSS_WEIGHT * (toward * f32(sp_ref[j]) - f32(next_ref[:, cols]) * away)
        slope_ref[j, :, :width] = slope.astype(jnp.bfloat16)
    distance = jnp.broadcast_to(1.0 - cosine, (rows, CARRY))
    high = f32(distance.astype(jnp.bfloat16))
    middle = f32((distance - high).astype(jnp.bfloat16))
    low = distance - high - middle
    lane = lax.broadcasted_iota(jnp.int32, (rows, CARRY), 1)
    carried = jnp.where(lane == 0, high, jnp.where(lane == 1, middle, low))
    carried = jnp.where(lane < 3, carried, 0.0).astype(jnp.bfloat16)
    for j in range(blocks):
        slope_ref[j, :, width:] = carried


def slopes(parts, x, sp):
    return pl.pallas_call(
        slope_kernel,
        out_shape=(
            jax.ShapeDtypeStruct(x.shape, jnp.bfloat16),
            jax.ShapeDtypeStruct((*sp.shape[:2], sp.shape[2] + CARRY), jnp.bfloat16),
        ),
        in_specs=[VM] * (len(parts) + 2),
        out_specs=(VM, VM),
        compiler_params=kernel_params(6),
        name="slopes",
    )(*parts, x, sp)


def stacked(refs, all_ref):
    for k, r in enumerate(refs):
        all_ref[:, k] = r[:, :, : all_ref.shape[3]]
    n_sec, n_y, rows, width = all_ref.shape
    return all_ref[...].reshape(n_sec * n_y * rows, width)


def blocks_of(sc_ref, size):
    core, xh = sc_ref[0], sc_ref[1]
    for at_x, at_c in ((xh, core), (xh, 1 - core), (1 - xh, core), (1 - xh, 1 - core)):
        yield pl.ds(pl.multiple_of((at_x * 2 + at_c) * size, size), size)


def student_proj_kernel(n_sends, sc_ref, *refs):
    distant, last_ref, keep_ref, send_refs = refs[:4], refs[4], refs[5], refs[6 : 6 + n_sends]
    near, sems = refs[6 + n_sends : -1], refs[-1]
    copies = fetched(distant, near, sems)
    tokens_ref, proj_refs = near[0], (*near[1:], last_ref)
    size = proj_refs[0].shape[0]
    total = None
    copies[0].wait()
    for cut, p, copy in zip(blocks_of(sc_ref, size), proj_refs, (*copies[1:], None)):
        if copy is not None:
            copy.wait()
        y = jnp.dot(tokens_ref[:, cut], p[...], preferred_element_type=jnp.float32)
        total = y if total is None else total + y
    n_sec, rows, block = keep_ref.shape
    total = total.reshape(n_sec, 1 + n_sends, rows, block)
    keep_ref[...] = total[:, 0]
    for k, out in enumerate(send_refs):
        out[...] = total[:, k + 1].astype(jnp.bfloat16)


def student_proj_part(scalars, tokens, proj, n_sec, n_y):
    n_tok, feats = tokens.shape
    rows, block = n_tok // (n_sec * n_y), proj[0].shape[1]
    keep = jax.ShapeDtypeStruct((n_sec, rows, block), jnp.float32)
    send = jax.ShapeDtypeStruct((n_sec, rows, block), jnp.bfloat16)
    inputs = (tokens, *proj[:3])
    return pl.pallas_call(
        functools.partial(student_proj_kernel, n_y - 1),
        out_shape=(keep,) + (send,) * (n_y - 1),
        in_specs=[SM] + [FAR] * len(inputs) + [VM],
        out_specs=(VM,) * n_y,
        scratch_shapes=[pltpu.VMEM(v.shape, v.dtype) for v in inputs]
        + [pltpu.SemaphoreType.DMA((len(inputs),))],
        compiler_params=kernel_params(14),
        cost_estimate=pl.CostEstimate(
            flops=2 * n_tok * feats * block,
            bytes_accessed=2 * (n_tok * feats + feats * block + n_tok * block),
            transcendentals=0,
        ),
        name="student_proj_part",
    )(scalars, *map(far, inputs), proj[3])


def turn_kernel(n, *refs):
    distant, outs, near, sems = refs[:n], refs[n : 2 * n], refs[2 * n : 3 * n], refs[-1]
    copies = fetched(distant, near, sems)
    for copy, v, out in zip(copies, near, outs):
        copy.wait()
        out[...] = v[...].T


def turned(values):
    return pl.pallas_call(
        functools.partial(turn_kernel, len(values)),
        out_shape=tuple(jax.ShapeDtypeStruct(v.shape[::-1], v.dtype) for v in values),
        in_specs=[FAR] * len(values),
        out_specs=(VM,) * len(values),
        scratch_shapes=[pltpu.VMEM(v.shape, v.dtype) for v in values]
        + [pltpu.SemaphoreType.DMA((len(values),))],
        compiler_params=kernel_params(14),
        name="turned",
    )(*map(far, values))


def gradients_kernel(n_y, sc_ref, *refs):
    slope_refs, tokens_ref, proj_refs = refs[:n_y], refs[n_y], refs[n_y + 1 : n_y + 5]
    gs_ref, loss_ref, away_far, away_near, stay_far, stay_near, all_ref = refs[n_y + 5 :]
    slope = stacked(slope_refs, all_ref)
    width, size = proj_refs[0].shape
    core, xh = sc_ref[0], sc_ref[1]
    for out, at_x, at_c in (
        (away_far, 1 - xh, 1 - core),
        (away_near, xh, 1 - core),
        (stay_far, 1 - xh, core),
        (stay_near, xh, core),
    ):
        cut = pl.ds(pl.multiple_of((at_x * 2 + at_c) * size, size), size)
        y = jnp.dot(tokens_ref[cut, :], slope, preferred_element_type=jnp.float32)
        out[...] = y.astype(out.dtype)
    for cut, p in zip(blocks_of(sc_ref, size), proj_refs):
        y = jnp.dot(slope, p[...], preferred_element_type=jnp.float32)
        n_z, n_xl, _, rows, _ = gs_ref.shape
        y = y.astype(jnp.bfloat16).reshape(n_z * n_xl, n_y, rows, size)
        for k in range(n_y):
            gs_ref[:, :, sc_ref[2] ^ k, :, cut] = y[:, k].reshape(n_z, n_xl, rows, size)
    loss = None
    for r in slope_refs:
        part = jnp.sum(f32(r[:, :, width:]), axis=(0, 1), keepdims=True)
        loss = part if loss is None else loss + part
    loss = jnp.sum(loss[0], axis=1, keepdims=True)
    loss_ref[...] = jnp.broadcast_to(loss, loss_ref.shape)


def gradients(scalars, slope, tokens_t, proj_t, n_z):
    n_y = len(slope)
    n_sec, rows = slope[0].shape[:2]
    width, size = proj_t[0].shape
    low = jax.ShapeDtypeStruct((size, width), jnp.bfloat16)
    high = jax.ShapeDtypeStruct((size, width), jnp.float32)
    inputs = (tokens_t, *proj_t)
    return pl.pallas_call(
        functools.partial(gradients_kernel, n_y),
        out_shape=(
            jax.ShapeDtypeStruct(
                (n_z, n_sec // n_z, n_y, rows, size * len(proj_t)), jnp.bfloat16
            ),
            jax.ShapeDtypeStruct((8, 128), jnp.float32),
            low,
            low,
            high,
            high,
        ),
        in_specs=[SM] + [VM] * (n_y + len(inputs)),
        out_specs=(VM,) * 6,
        scratch_shapes=[pltpu.VMEM((n_sec, n_y, rows, width), jnp.bfloat16)],
        compiler_params=kernel_params(10),
        name="gradients",
    )(scalars, *slope, *inputs)


def leading_sum_kernel(g_ref, o_ref):
    total = f32(g_ref[0])
    for s in range(1, g_ref.shape[0]):
        total += f32(g_ref[s])
    o_ref[...] = total.astype(o_ref.dtype)


def leading_sum(g):
    return pl.pallas_call(
        leading_sum_kernel,
        out_shape=jax.ShapeDtypeStruct(g.shape[1:], g.dtype),
        in_specs=[VM],
        out_specs=VM,
        compiler_params=kernel_params(6),
        name="leading_sum",
    )(g)


def place_kernel(g_ref, o_ref):
    n_xl, n_y, _, feats = g_ref.shape
    for k in range(n_y):
        total = f32(g_ref[0, k])
        for s in range(1, n_xl):
            total += f32(g_ref[s, k])
        o_ref[:, k * feats : (k + 1) * feats] = total


def placed_feats(g):
    _, n_y, rows, feats = g.shape
    return pl.pallas_call(
        place_kernel,
        out_shape=jax.ShapeDtypeStruct((rows, feats * n_y), jnp.float32),
        in_specs=[VM],
        out_specs=VM,
        compiler_params=kernel_params(4),
        name="placed_feats",
    )(g)


def tied(*values):
    return lax.optimization_barrier(values)


def to_columns(value, n_y):
    return [value] + [swap(value, "y", k) for k in range(1, n_y)]


def step(
    teacher_rows,
    norm_gain,
    query_weight,
    keys_values,
    output_weight,
    doc_start,
    student_rows,
    projector,
):
    core = lax.axis_index("c").astype(jnp.int32)
    xh = lax.axis_index("xh").astype(jnp.int32)
    y = lax.axis_index("y").astype(jnp.int32)
    n_sec = lax.axis_size(SEC)
    n_y = lax.axis_size("y")
    n_tp = lax.axis_size(TP)
    x = teacher_rows[0]
    rows, width = x.shape
    scalars = jnp.stack([core, xh, y, doc_start[0]])

    feats = student_rows.shape[2] // n_y
    picked = [
        lax.dynamic_slice_in_dim(student_rows[0], (y ^ k) * feats, feats, axis=1)
        for k in range(n_y)
    ]
    picked = [picked[0]] + [swap(picked[k], "y", k) for k in range(1, n_y)]
    proj = [projector, swap(projector, "c", 1), swap(projector, "xh", 1)]

    normed = normalize(x, norm_gain)
    y1, y3 = swap(normed, "y", 1), swap(normed, "y", 3)
    across = swap(normed, "xh", 1)
    y2 = swap(normed, "y", 2)
    own = [normed, y1, y2, y3]
    own += [across, swap(across, "y", 1), swap(across, "y", 2), swap(across, "y", 3)]
    other = [swap(v, "c", 1) for v in own]
    kv_mine = jnp.swapaxes(keys_values[0], 1, 2)
    kv_other = swap(kv_mine, "c", 1)

    mine, _ = tied(jnp.stack(picked), normed)
    tokens = exchange(jnp.broadcast_to(mine, (n_sec, *mine.shape)), SEC)
    n_tok = n_sec * n_y * rows
    tokens = tokens.reshape(n_tok, feats)

    mixed, to_other, kept = attention(
        scalars, other + own, query_weight[0], kv_mine, kv_other, output_weight[0]
    )

    proj[2], mixed = tied(proj[2], mixed)
    proj.append(swap(proj[2], "c", 1))
    half = width // 2
    sides = [(kept, to_other, swap(to_other, "c", 1))]

    keep, *sends = student_proj_part(scalars, tokens, proj, n_sec, n_y)
    mixed, keep = tied(mixed, keep)
    got = [swap(sends[k - 1], "y", k) for k in range(1, n_y)]
    to_other, kept = project(mixed, output_weight[0], half, half)
    sides.append((kept, to_other, swap(to_other, "c", 1)))

    pieces = add_pieces([s[0] for s in sides], [s[2] for s in sides], 2 * n_y)
    near, away = list(pieces[:n_y]), list(pieces[n_y:])
    relayed = swap(away[2], "xh", 1)
    away = sum_of((away[0], swap(away[1], "y", 1), swap(away[3], "y", 3)), jnp.bfloat16)
    away = swap(away, "xh", 1)
    relayed = swap(sum_of((near[2], relayed), jnp.bfloat16), "y", 2)
    parts = (near[0], swap(near[1], "y", 1), swap(near[3], "y", 3), relayed, away)

    sp = sum_of((keep, *got), jnp.bfloat16)
    sp = exchange(sp, SEC)
    teacher_next, slope = slopes(parts, x, sp)

    slope = exchange(slope, SEC)
    slope, tokens = tied(slope, tokens)
    slope = to_columns(slope, n_y)
    tokens_t, *proj_t = turned((tokens, *proj))
    grad_s, loss, away_far, away_near, stay_far, stay_near = gradients(
        scalars, slope, tokens_t, proj_t, lax.axis_size("z")
    )
    grad_s = exchange(grad_s, "z")
    loss = loss + swap(loss, "c", 1)
    away_far = swap(away_far, "c", 1)
    away_near = swap(away_near, "c", 1)
    loss = loss + swap(loss, "xh", 1)
    across = swap(sum_of((stay_far, away_far), jnp.bfloat16), "xh", 1)
    nearly = sum_of((stay_near, away_near), jnp.float32)
    loss = loss[:1, :1] / (n_sec * n_tp * rows)
    grad_s, loss, nearly = tied(grad_s, loss, nearly)
    grad_s = leading_sum(grad_s)
    shape = grad_s.shape
    grad_s = exchange(grad_s.reshape(-1, *shape[2:]), ("xl", "y")).reshape(shape)
    grad_projector = sum_of((nearly, across), jnp.float32)
    grad_s, grad_projector = tied(grad_s, grad_projector)
    grad_student = placed_feats(grad_s)
    return (teacher_next[None], loss[0, 0], grad_student[None], grad_projector)


def solution(mesh):
    fine = Mesh(mesh.devices.reshape(4, 2, 4, 2, 2), ("z", "xl", "y", "xh", "c"))
    placed = (
        P(SEC, TP, None),
        P(SEC, None),
        P(SEC, None, TP),
        P(SEC, None, None, TP),
        P(SEC, TP, None),
        P(SEC),
        P(SEC, TP, None),
        P(TP, SEC),
    )
    return jax.shard_map(
        step,
        mesh=fine,
        in_specs=placed,
        out_specs=(P(SEC, TP, None), P(), P(SEC, TP, None), P(TP, SEC)),
        check_vma=False,
    )
```

```python
import functools
import math

import jax
import jax.numpy as jnp
from jax import lax
from jax.experimental import pallas as pl
from jax.experimental.pallas import tpu as pltpu
from jax.sharding import Mesh
from jax.sharding import PartitionSpec as P

HD = 128
LOSS_WEIGHT = 64.0
NORM_EPS = 1e-05
COS_EPS = 1e-06
CARRY = 128
SEC = ("z", "xl")
TP = ("y", "xh", "c")

VM = pl.BlockSpec(memory_space=pltpu.VMEM)
SM = pl.BlockSpec(memory_space=pltpu.SMEM)
FAR = pl.BlockSpec(memory_space=pltpu.HBM)


def exchange(pieces, axes):
    return lax.all_to_all(pieces, axes, split_axis=0, concat_axis=0, tiled=True)


def swap(value, axis, apart=1):
    count = lax.axis_size(axis)
    return lax.ppermute(value, axis, [(i, i ^ apart) for i in range(count)])


def f32(value):
    return value.astype(jnp.float32)


def kernel_params(mib):
    return pltpu.CompilerParams(vmem_limit_bytes=mib * 2**20)


def far(value):
    return pltpu.with_memory_space_constraint(value, pltpu.HBM)


def fetched(sources, targets, sems):
    copies = [
        pltpu.make_async_copy(s, t, sems.at[i]) for i, (s, t) in enumerate(zip(sources, targets))
    ]
    for copy in copies:
        copy.start()
    return copies


def norm_kernel(x_far, gain_far, o_ref, x_ref, gain_ref, sems):
    for copy in fetched((x_far, gain_far), (x_ref, gain_ref), sems):
        copy.wait()
    x = f32(x_ref[...])
    mean_square = jnp.mean(x * x, axis=1, keepdims=True)
    o_ref[...] = (x * lax.rsqrt(mean_square + NORM_EPS) * gain_ref[...]).astype(jnp.bfloat16)


def normalize(x, gain):
    return pl.pallas_call(
        norm_kernel,
        out_shape=jax.ShapeDtypeStruct(x.shape, jnp.bfloat16),
        in_specs=[FAR, FAR],
        out_specs=VM,
        scratch_shapes=[
            pltpu.VMEM(x.shape, x.dtype),
            pltpu.VMEM(gain.shape, gain.dtype),
            pltpu.SemaphoreType.DMA((2,)),
        ],
        compiler_params=kernel_params(4),
        name="normalize",
    )(far(x), far(gain))


def attention_kernel(n_shards, chunk, sc_ref, *refs):
    n_far = n_shards // 2
    far_refs = refs[:n_far]
    wq_hbm, kva_hbm, kvb_hbm, wo_hbm, o_ref, other_ref, own_ref = refs[n_shards : n_shards + 7]
    q_acc, kv_acc, wq_ref, kva_ref, kvb_ref, wo_ref, held_ref, sems, out_sem, held_sems = refs[
        n_shards + 7 :
    ]
    own_refs = refs[n_far:n_shards]
    per, depth = own_refs[0].shape
    rows = n_shards * per
    half = rows // 2
    dh = kva_ref.shape[1]
    steps = depth // chunk

    def fetch(step):
        cut = pl.ds(pl.multiple_of(step * chunk, chunk), chunk)
        return (
            pltpu.make_async_copy(wq_hbm.at[cut, :], wq_ref.at[cut, :], sems.at[0, step]),
            pltpu.make_async_copy(kva_hbm.at[:, :, cut], kva_ref.at[:, :, cut], sems.at[1, step]),
            pltpu.make_async_copy(kvb_hbm.at[:, :, cut], kvb_ref.at[:, :, cut], sems.at[2, step]),
            *(
                pltpu.make_async_copy(
                    r.at[:, cut], held_ref.at[i * per : (i + 1) * per, cut], held_sems.at[i, step]
                )
                for i, r in enumerate(far_refs)
            ),
        )

    for step in range(steps):
        for copy in fetch(step):
            copy.start()
    half_cols = own_ref.shape[1]
    out_copy = pltpu.make_async_copy(wo_hbm.at[:, :half_cols], wo_ref, out_sem.at[0])
    out_copy.start()
    q_acc[...] = jnp.zeros_like(q_acc)
    kv_acc[...] = jnp.zeros_like(kv_acc)

    @pl.loop(0, steps)
    def _(step):
        for copy in fetch(step):
            copy.wait()
        cut = pl.ds(pl.multiple_of(step * chunk, chunk), chunk)
        x = jnp.concatenate([held_ref[:, cut], *(r[:, cut] for r in own_refs)], axis=0)
        wkv = jnp.concatenate(
            [kva_ref[0, :, cut], kvb_ref[0, :, cut], kva_ref[1, :, cut], kvb_ref[1, :, cut]],
            axis=0,
        )
        q_acc[...] += jnp.dot(x, wq_ref[cut, :], preferred_element_type=jnp.float32)
        kv_acc[...] += lax.dot_general(
            x, wkv, (((1,), (1,)), ((), ())), preferred_element_type=jnp.float32
        )

    core, xh, y, first_new = sc_ref[0], sc_ref[1], sc_ref[2], sc_ref[3]
    low = core == 0
    keys = kv_acc[:, :HD]
    values = kv_acc[:, HD:]
    keys = jnp.where(low, keys, pltpu.roll(keys, dh, axis=1)).astype(jnp.bfloat16)
    values = jnp.where(low, values, pltpu.roll(values, dh, axis=1)).astype(jnp.bfloat16)

    def place(shape, dim):
        i = lax.broadcasted_iota(jnp.int32, shape, dim)
        side = jnp.where(i < half, 1 - core, core)
        chip_x = ((i >> 6) & 1) ^ xh
        chip_y = ((i >> 4) & 3) ^ y
        return (chip_y * 4 + chip_x * 2 + side) * per + (i & (per - 1))

    row, col = place((rows, rows), 0), place((rows, rows), 1)
    visible = (col <= row) & ((col >= first_new) == (row >= first_new))
    scale = 1.0 / math.sqrt(HD)
    for h in range(q_acc.shape[1] // HD):
        head = slice(h * HD, (h + 1) * HD)
        q = q_acc[:, head].astype(jnp.bfloat16)
        scores = (
            lax.dot_general(q, keys, (((1,), (1,)), ((), ())), preferred_element_type=jnp.float32)
            * scale
        )
        scores = jnp.where(visible, scores, -1e30)
        top = jnp.max(scores, axis=1, keepdims=True)
        expo = jnp.where(visible, jnp.exp(scores - top), 0.0)
        weights = (expo / jnp.sum(expo, axis=1, keepdims=True)).astype(jnp.bfloat16)
        mixed = jnp.dot(weights, values, preferred_element_type=jnp.float32)
        o_ref[:, head] = mixed.astype(jnp.bfloat16)
    out_copy.wait()
    for cut in (slice(i, i + 512) for i in range(0, half_cols, 512)):
        y = jnp.dot(o_ref[...], wo_ref[:, cut], preferred_element_type=jnp.float32)
        other_ref[:, cut] = y[:half].astype(jnp.bfloat16)
        own_ref[:, cut] = y[half:].astype(jnp.bfloat16)


def attention(scalars, shards_in, wq, kv_mine, kv_other, wo, chunk=1024):
    per, depth = shards_in[0].shape
    n_shards = len(shards_in)
    rows = per * n_shards
    cols = wq.shape[1]
    dh = kv_mine.shape[1]
    half_cols = wo.shape[1] // 2
    part = jax.ShapeDtypeStruct((rows // 2, half_cols), jnp.bfloat16)
    return pl.pallas_call(
        functools.partial(attention_kernel, n_shards, chunk),
        out_shape=(jax.ShapeDtypeStruct((rows, cols), jnp.bfloat16), part, part),
        in_specs=[SM] + [FAR] * (n_shards // 2) + [VM] * (n_shards // 2) + [FAR] * 4,
        out_specs=(VM,) * 3,
        scratch_shapes=[
            pltpu.VMEM((rows, cols), jnp.float32),
            pltpu.VMEM((rows, 4 * dh), jnp.float32),
            pltpu.VMEM(wq.shape, jnp.bfloat16),
            pltpu.VMEM(kv_mine.shape, jnp.bfloat16),
            pltpu.VMEM(kv_other.shape, jnp.bfloat16),
            pltpu.VMEM((cols, half_cols), jnp.bfloat16),
            pltpu.VMEM((rows // 2, depth), jnp.bfloat16),
            pltpu.SemaphoreType.DMA((3, depth // chunk)),
            pltpu.SemaphoreType.DMA((1,)),
            pltpu.SemaphoreType.DMA((n_shards // 2, depth // chunk)),
        ],
        compiler_params=kernel_params(28),
        cost_estimate=pl.CostEstimate(
            flops=2 * rows * depth * (cols + 4 * dh),
            bytes_accessed=2 * (rows * depth + depth * (cols + 4 * dh)),
            transcendentals=4 * rows * rows,
        ),
        name="attention",
    )(scalars, *map(far, shards_in[: n_shards // 2]), *shards_in[n_shards // 2 :], far(wq), far(kv_mine), far(kv_other), far(wo))


def project_kernel(base, chunk, m_ref, w_hbm, other_ref, own_ref, w_ref, sems):
    half, cols = other_ref.shape
    copies = []
    for step in range(cols // chunk):
        copies.append(
            pltpu.make_async_copy(
                w_hbm.at[:, base + step * chunk : base + (step + 1) * chunk],
                w_ref.at[:, step * chunk : (step + 1) * chunk],
                sems.at[step],
            )
        )
        copies[-1].start()
    for step, copy in enumerate(copies):
        copy.wait()
        cut = slice(step * chunk, (step + 1) * chunk)
        y = jnp.dot(m_ref[...], w_ref[:, cut], preferred_element_type=jnp.float32)
        other_ref[:, cut] = y[:half].astype(jnp.bfloat16)
        own_ref[:, cut] = y[half:].astype(jnp.bfloat16)


def project(mixed, w, base, cols, chunk=512):
    rows, depth = mixed.shape
    out = jax.ShapeDtypeStruct((rows // 2, cols), jnp.bfloat16)
    return pl.pallas_call(
        functools.partial(project_kernel, base, chunk),
        out_shape=(out, out),
        in_specs=[VM, FAR],
        out_specs=(VM, VM),
        scratch_shapes=[
            pltpu.VMEM((depth, cols), jnp.bfloat16),
            pltpu.SemaphoreType.DMA((cols // chunk,)),
        ],
        compiler_params=kernel_params(12),
        cost_estimate=pl.CostEstimate(
            flops=2 * rows * depth * cols,
            bytes_accessed=2 * (rows * depth + depth * cols + rows * cols),
            transcendentals=0,
        ),
        name="project",
    )(mixed, far(w))


def add_kernel(n, *refs):
    outs = refs[2 * n :]
    per = outs[0].shape[0]
    width = refs[0].shape[1]
    for i, out in enumerate(outs):
        cut = slice(i * per, (i + 1) * per)
        for j in range(n):
            total = f32(refs[j][cut, :]) + f32(refs[n + j][cut, :])
            out[:, j * width : (j + 1) * width] = total.astype(jnp.bfloat16)


def add_pieces(kept, arrived, count):
    rows, cols = kept[0].shape
    out = jax.ShapeDtypeStruct((rows // count, cols * len(kept)), jnp.bfloat16)
    return pl.pallas_call(
        functools.partial(add_kernel, len(kept)),
        out_shape=(out,) * count,
        in_specs=[VM] * (2 * len(kept)),
        out_specs=(VM,) * count,
        compiler_params=kernel_params(4),
        name="add_pieces",
    )(*kept, *arrived)


def sum_kernel(*refs):
    total = f32(refs[0][...])
    for r in refs[1:-1]:
        total += f32(r[...])
    refs[-1][...] = total.astype(refs[-1].dtype)


def sum_of(arrays, dtype):
    return pl.pallas_call(
        sum_kernel,
        out_shape=jax.ShapeDtypeStruct(arrays[0].shape, dtype),
        in_specs=[VM] * len(arrays),
        out_specs=VM,
        compiler_params=kernel_params(4),
        name="sum_of",
    )(*arrays)


def slope_kernel(*refs):
    parts = refs[:-4]
    x_ref, sp_ref, next_ref, slope_ref = refs[-4:]
    blocks, rows, width = sp_ref.shape
    inner = jnp.zeros((rows, 1), jnp.float32)
    own_sq = jnp.zeros((rows, 1), jnp.float32)
    target_sq = jnp.zeros((rows, 1), jnp.float32)
    for j in range(blocks):
        cols = slice(j * width, (j + 1) * width)
        total = f32(parts[0][:, cols])
        for p in parts[1:]:
            total += f32(p[:, cols])
        new = (f32(x_ref[:, cols]) + total).astype(jnp.bfloat16)
        next_ref[:, cols] = new
        target = f32(new)
        sp = f32(sp_ref[j])
        inner += jnp.sum(sp * target, axis=1, keepdims=True)
        own_sq += jnp.sum(sp * sp, axis=1, keepdims=True)
        target_sq += jnp.sum(target * target, axis=1, keepdims=True)
    inv_own = lax.rsqrt(own_sq + COS_EPS)
    inv_target = lax.rsqrt(target_sq + COS_EPS)
    cosine = inner * inv_own * inv_target
    toward = inner * inv_target * inv_own * inv_own * inv_own
    away = inv_own * inv_target
    for j in range(blocks):
        cols = slice(j * width, (j + 1) * width)
        slope = LOSS_WEIGHT * (toward * f32(sp_ref[j]) - f32(next_ref[:, cols]) * away)
        slope_ref[j, :, :width] = slope.astype(jnp.bfloat16)
    distance = jnp.broadcast_to(1.0 - cosine, (rows, CARRY))
    high = f32(distance.astype(jnp.bfloat16))
    middle = f32((distance - high).astype(jnp.bfloat16))
    low = distance - high - middle
    lane = lax.broadcasted_iota(jnp.int32, (rows, CARRY), 1)
    carried = jnp.where(lane == 0, high, jnp.where(lane == 1, middle, low))
    carried = jnp.where(lane < 3, carried, 0.0).astype(jnp.bfloat16)
    for j in range(blocks):
        slope_ref[j, :, width:] = carried


def slopes(parts, x, sp):
    return pl.pallas_call(
        slope_kernel,
        out_shape=(
            jax.ShapeDtypeStruct(x.shape, jnp.bfloat16),
            jax.ShapeDtypeStruct((*sp.shape[:2], sp.shape[2] + CARRY), jnp.bfloat16),
        ),
        in_specs=[VM] * (len(parts) + 2),
        out_specs=(VM, VM),
        compiler_params=kernel_params(6),
        name="slopes",
    )(*parts, x, sp)


def stacked(refs, all_ref):
    for k, r in enumerate(refs):
        all_ref[:, k] = r[:, :, : all_ref.shape[3]]
    n_sec, n_y, rows, width = all_ref.shape
    return all_ref[...].reshape(n_sec * n_y * rows, width)


def blocks_of(sc_ref, size):
    core, xh = sc_ref[0], sc_ref[1]
    for at_x, at_c in ((xh, core), (xh, 1 - core), (1 - xh, core), (1 - xh, 1 - core)):
        yield pl.ds(pl.multiple_of((at_x * 2 + at_c) * size, size), size)


def student_proj_kernel(n_sends, sc_ref, *refs):
    distant, last_ref, keep_ref, send_refs = refs[:4], refs[4], refs[5], refs[6 : 6 + n_sends]
    near, sems = refs[6 + n_sends : -1], refs[-1]
    copies = fetched(distant, near, sems)
    tokens_ref, proj_refs = near[0], (*near[1:], last_ref)
    size = proj_refs[0].shape[0]
    total = None
    copies[0].wait()
    for cut, p, copy in zip(blocks_of(sc_ref, size), proj_refs, (*copies[1:], None)):
        if copy is not None:
            copy.wait()
        y = jnp.dot(tokens_ref[:, cut], p[...], preferred_element_type=jnp.float32)
        total = y if total is None else total + y
    n_sec, rows, block = keep_ref.shape
    total = total.reshape(n_sec, 1 + n_sends, rows, block)
    keep_ref[...] = total[:, 0]
    for k, out in enumerate(send_refs):
        out[...] = total[:, k + 1].astype(jnp.bfloat16)


def student_proj_part(scalars, tokens, proj, n_sec, n_y):
    n_tok, feats = tokens.shape
    rows, block = n_tok // (n_sec * n_y), proj[0].shape[1]
    keep = jax.ShapeDtypeStruct((n_sec, rows, block), jnp.float32)
    send = jax.ShapeDtypeStruct((n_sec, rows, block), jnp.bfloat16)
    inputs = (tokens, *proj[:3])
    return pl.pallas_call(
        functools.partial(student_proj_kernel, n_y - 1),
        out_shape=(keep,) + (send,) * (n_y - 1),
        in_specs=[SM] + [FAR] * len(inputs) + [VM],
        out_specs=(VM,) * n_y,
        scratch_shapes=[pltpu.VMEM(v.shape, v.dtype) for v in inputs]
        + [pltpu.SemaphoreType.DMA((len(inputs),))],
        compiler_params=kernel_params(14),
        cost_estimate=pl.CostEstimate(
            flops=2 * n_tok * feats * block,
            bytes_accessed=2 * (n_tok * feats + feats * block + n_tok * block),
            transcendentals=0,
        ),
        name="student_proj_part",
    )(scalars, *map(far, inputs), proj[3])


def turn_kernel(n, *refs):
    distant, outs, near, sems = refs[:n], refs[n : 2 * n], refs[2 * n : 3 * n], refs[-1]
    copies = fetched(distant, near, sems)
    for copy, v, out in zip(copies, near, outs):
        copy.wait()
        out[...] = v[...].T


def turned(values):
    return pl.pallas_call(
        functools.partial(turn_kernel, len(values)),
        out_shape=tuple(jax.ShapeDtypeStruct(v.shape[::-1], v.dtype) for v in values),
        in_specs=[FAR] * len(values),
        out_specs=(VM,) * len(values),
        scratch_shapes=[pltpu.VMEM(v.shape, v.dtype) for v in values]
        + [pltpu.SemaphoreType.DMA((len(values),))],
        compiler_params=kernel_params(14),
        name="turned",
    )(*map(far, values))


def gradients_kernel(n_y, sc_ref, *refs):
    slope_refs, tokens_ref, proj_refs = refs[:n_y], refs[n_y], refs[n_y + 1 : n_y + 5]
    loss_ref, away_far, away_near, stay_far, stay_near = refs[n_y + 5 : n_y + 10]
    piece_refs, all_ref, gs_ref = refs[n_y + 10 : -2], refs[-2], refs[-1]
    slope = stacked(slope_refs, all_ref)
    width, size = proj_refs[0].shape
    core, xh = sc_ref[0], sc_ref[1]
    for out, at_x, at_c in (
        (away_far, 1 - xh, 1 - core),
        (away_near, xh, 1 - core),
        (stay_far, 1 - xh, core),
        (stay_near, xh, core),
    ):
        cut = pl.ds(pl.multiple_of((at_x * 2 + at_c) * size, size), size)
        y = jnp.dot(tokens_ref[cut, :], slope, preferred_element_type=jnp.float32)
        out[...] = y.astype(out.dtype)
    for cut, p in zip(blocks_of(sc_ref, size), proj_refs):
        y = jnp.dot(slope, p[...], preferred_element_type=jnp.float32)
        n_z, n_xl, _, rows, _ = gs_ref.shape
        y = y.astype(jnp.bfloat16).reshape(n_z * n_xl, n_y, rows, size)
        for k in range(n_y):
            gs_ref[:, :, sc_ref[2] ^ k, :, cut] = y[:, k].reshape(n_z, n_xl, rows, size)
    for k, out in enumerate(piece_refs):
        out[...] = gs_ref[sc_ref[4] ^ k]
    loss = None
    for r in slope_refs:
        part = jnp.sum(f32(r[:, :, width:]), axis=(0, 1), keepdims=True)
        loss = part if loss is None else loss + part
    loss = jnp.sum(loss[0], axis=1, keepdims=True)
    loss_ref[...] = jnp.broadcast_to(loss, loss_ref.shape)


def gradients(scalars, slope, tokens_t, proj_t, n_z):
    n_y = len(slope)
    n_sec, rows = slope[0].shape[:2]
    width, size = proj_t[0].shape
    low = jax.ShapeDtypeStruct((size, width), jnp.bfloat16)
    high = jax.ShapeDtypeStruct((size, width), jnp.float32)
    shape = (n_z, n_sec // n_z, n_y, rows, size * len(proj_t))
    piece = jax.ShapeDtypeStruct(shape[1:], jnp.bfloat16)
    inputs = (tokens_t, *proj_t)
    return pl.pallas_call(
        functools.partial(gradients_kernel, n_y),
        out_shape=(
            jax.ShapeDtypeStruct((8, 128), jnp.float32),
            low,
            low,
            high,
            high,
            *(piece,) * n_z,
        ),
        in_specs=[SM] + [VM] * (n_y + len(inputs)),
        out_specs=(VM,) * (5 + n_z),
        scratch_shapes=[
            pltpu.VMEM((n_sec, n_y, rows, width), jnp.bfloat16),
            pltpu.VMEM(shape, jnp.bfloat16),
        ],
        compiler_params=kernel_params(12),
        name="gradients",
    )(scalars, *slope, *inputs)


def place_kernel(g_ref, o_ref):
    n_xl, n_y, _, feats = g_ref.shape
    for k in range(n_y):
        total = f32(g_ref[0, k])
        for s in range(1, n_xl):
            total += f32(g_ref[s, k])
        o_ref[:, k * feats : (k + 1) * feats] = total


def placed_feats(g):
    _, n_y, rows, feats = g.shape
    return pl.pallas_call(
        place_kernel,
        out_shape=jax.ShapeDtypeStruct((rows, feats * n_y), jnp.float32),
        in_specs=[VM],
        out_specs=VM,
        compiler_params=kernel_params(4),
        name="placed_feats",
    )(g)


def tied(*values):
    return lax.optimization_barrier(values)


def to_columns(value, n_y):
    return [value] + [swap(value, "y", k) for k in range(1, n_y)]


def step(
    teacher_rows,
    norm_gain,
    query_weight,
    keys_values,
    output_weight,
    doc_start,
    student_rows,
    projector,
):
    core = lax.axis_index("c").astype(jnp.int32)
    xh = lax.axis_index("xh").astype(jnp.int32)
    y = lax.axis_index("y").astype(jnp.int32)
    n_sec = lax.axis_size(SEC)
    n_y = lax.axis_size("y")
    n_tp = lax.axis_size(TP)
    x = teacher_rows[0]
    rows, width = x.shape
    z = lax.axis_index("z").astype(jnp.int32)
    scalars = jnp.stack([core, xh, y, doc_start[0], z])

    feats = student_rows.shape[2] // n_y
    picked = [
        lax.dynamic_slice_in_dim(student_rows[0], (y ^ k) * feats, feats, axis=1)
        for k in range(n_y)
    ]
    picked = [picked[0]] + [swap(picked[k], "y", k) for k in range(1, n_y)]
    proj = [projector, swap(projector, "c", 1), swap(projector, "xh", 1)]

    normed = normalize(x, norm_gain)
    y1, y3 = swap(normed, "y", 1), swap(normed, "y", 3)
    across = swap(normed, "xh", 1)
    y2 = swap(normed, "y", 2)
    own = [normed, y1, y2, y3]
    own += [across, swap(across, "y", 1), swap(across, "y", 2), swap(across, "y", 3)]
    other = [swap(v, "c", 1) for v in own]
    kv_mine = jnp.swapaxes(keys_values[0], 1, 2)
    kv_other = swap(kv_mine, "c", 1)

    mine, _ = tied(jnp.stack(picked), normed)
    tokens = exchange(jnp.broadcast_to(mine, (n_sec, *mine.shape)), SEC)
    n_tok = n_sec * n_y * rows
    tokens = tokens.reshape(n_tok, feats)

    mixed, to_other, kept = attention(
        scalars, other + own, query_weight[0], kv_mine, kv_other, output_weight[0]
    )

    proj[2], mixed = tied(proj[2], mixed)
    proj.append(swap(proj[2], "c", 1))
    half = width // 2
    sides = [(kept, to_other, swap(to_other, "c", 1))]

    keep, *sends = student_proj_part(scalars, tokens, proj, n_sec, n_y)
    mixed, keep = tied(mixed, keep)
    got = [swap(sends[k - 1], "y", k) for k in range(1, n_y)]
    to_other, kept = project(mixed, output_weight[0], half, half)
    sides.append((kept, to_other, swap(to_other, "c", 1)))

    pieces = add_pieces([s[0] for s in sides], [s[2] for s in sides], 2 * n_y)
    near, away = list(pieces[:n_y]), list(pieces[n_y:])
    relayed = swap(away[2], "xh", 1)
    away = sum_of((away[0], swap(away[1], "y", 1), swap(away[3], "y", 3)), jnp.bfloat16)
    away = swap(away, "xh", 1)
    relayed = swap(sum_of((near[2], relayed), jnp.bfloat16), "y", 2)
    parts = (near[0], swap(near[1], "y", 1), swap(near[3], "y", 3), relayed, away)

    sp = sum_of((keep, *got), jnp.bfloat16)
    sp = exchange(sp, SEC)
    teacher_next, slope = slopes(parts, x, sp)

    slope = exchange(slope, SEC)
    slope, tokens = tied(slope, tokens)
    slope = to_columns(slope, n_y)
    tokens_t, *proj_t = turned((tokens, *proj))
    loss, away_far, away_near, stay_far, stay_near, *grad_s = gradients(
        scalars, slope, tokens_t, proj_t, lax.axis_size("z")
    )
    for k in range(1, len(grad_s)):
        grad_s[k] = swap(grad_s[k], "z", k)
    loss = loss + swap(loss, "c", 1)
    away_far = swap(away_far, "c", 1)
    away_near = swap(away_near, "c", 1)
    loss = loss + swap(loss, "xh", 1)
    across = swap(sum_of((stay_far, away_far), jnp.bfloat16), "xh", 1)
    nearly = sum_of((stay_near, away_near), jnp.float32)
    loss = loss[:1, :1] / (n_sec * n_tp * rows)
    grad_s[2], nearly = tied(grad_s[2], nearly)
    grad_s = sum_of(grad_s, jnp.bfloat16)
    shape = grad_s.shape
    grad_s = exchange(grad_s.reshape(-1, *shape[2:]), ("xl", "y")).reshape(shape)
    grad_projector = sum_of((nearly, across), jnp.float32)
    grad_s, grad_projector = tied(grad_s, grad_projector)
    grad_student = placed_feats(grad_s)
    return (teacher_next[None], loss[0, 0], grad_student[None], grad_projector)


def solution(mesh):
    fine = Mesh(mesh.devices.reshape(4, 2, 4, 2, 2), ("z", "xl", "y", "xh", "c"))
    placed = (
        P(SEC, TP, None),
        P(SEC, None),
        P(SEC, None, TP),
        P(SEC, None, None, TP),
        P(SEC, TP, None),
        P(SEC),
        P(SEC, TP, None),
        P(TP, SEC),
    )
    return jax.shard_map(
        step,
        mesh=fine,
        in_specs=placed,
        out_specs=(P(SEC, TP, None), P(), P(SEC, TP, None), P(TP, SEC)),
        check_vma=False,
    )
```

```python
import functools
import math

import jax
import jax.numpy as jnp
from jax import lax
from jax.experimental import pallas as pl
from jax.experimental.pallas import tpu as pltpu
from jax.sharding import Mesh
from jax.sharding import PartitionSpec as P

HD = 128
LOSS_WEIGHT = 64.0
NORM_EPS = 1e-05
COS_EPS = 1e-06
CARRY = 128
SEC = ("z", "xl")
TP = ("y", "xh", "c")

VM = pl.BlockSpec(memory_space=pltpu.VMEM)
SM = pl.BlockSpec(memory_space=pltpu.SMEM)
FAR = pl.BlockSpec(memory_space=pltpu.HBM)


def exchange(pieces, axes):
    return lax.all_to_all(pieces, axes, split_axis=0, concat_axis=0, tiled=True)


def swap(value, axis, apart=1):
    count = lax.axis_size(axis)
    return lax.ppermute(value, axis, [(i, i ^ apart) for i in range(count)])


def f32(value):
    return value.astype(jnp.float32)


def kernel_params(mib):
    return pltpu.CompilerParams(vmem_limit_bytes=mib * 2**20)


def far(value):
    return pltpu.with_memory_space_constraint(value, pltpu.HBM)


def fetched(sources, targets, sems):
    copies = [
        pltpu.make_async_copy(s, t, sems.at[i]) for i, (s, t) in enumerate(zip(sources, targets))
    ]
    for copy in copies:
        copy.start()
    return copies


def norm_kernel(x_far, gain_far, o_ref, x_ref, gain_ref, sems):
    for copy in fetched((x_far, gain_far), (x_ref, gain_ref), sems):
        copy.wait()
    x = f32(x_ref[...])
    mean_square = jnp.mean(x * x, axis=1, keepdims=True)
    o_ref[...] = (x * lax.rsqrt(mean_square + NORM_EPS) * gain_ref[...]).astype(jnp.bfloat16)


def normalize(x, gain):
    return pl.pallas_call(
        norm_kernel,
        out_shape=jax.ShapeDtypeStruct(x.shape, jnp.bfloat16),
        in_specs=[FAR, FAR],
        out_specs=VM,
        scratch_shapes=[
            pltpu.VMEM(x.shape, x.dtype),
            pltpu.VMEM(gain.shape, gain.dtype),
            pltpu.SemaphoreType.DMA((2,)),
        ],
        compiler_params=kernel_params(4),
        name="normalize",
    )(far(x), far(gain))


def attention_kernel(n_shards, chunk, sc_ref, *refs):
    n_far = n_shards // 2
    far_refs = refs[:n_far]
    wq_hbm, kva_hbm, kvb_hbm, wo_hbm, other_ref, own_ref, o_ref = refs[n_shards : n_shards + 7]
    q_acc, kv_acc, wq_ref, kva_ref, kvb_ref, wo_ref, held_ref, sems, out_sem, held_sems = refs[
        n_shards + 7 :
    ]
    own_refs = refs[n_far:n_shards]
    per, depth = own_refs[0].shape
    rows = n_shards * per
    half = rows // 2
    dh = kva_ref.shape[1]
    steps = depth // chunk

    def fetch(step):
        cut = pl.ds(pl.multiple_of(step * chunk, chunk), chunk)
        return (
            pltpu.make_async_copy(wq_hbm.at[cut, :], wq_ref.at[cut, :], sems.at[0, step]),
            pltpu.make_async_copy(kva_hbm.at[:, :, cut], kva_ref.at[:, :, cut], sems.at[1, step]),
            pltpu.make_async_copy(kvb_hbm.at[:, :, cut], kvb_ref.at[:, :, cut], sems.at[2, step]),
            *(
                pltpu.make_async_copy(
                    r.at[:, cut], held_ref.at[i * per : (i + 1) * per, cut], held_sems.at[i, step]
                )
                for i, r in enumerate(far_refs)
            ),
        )

    for step in range(steps):
        for copy in fetch(step):
            copy.start()
    out_cols = own_ref.shape[1]
    out_copy = pltpu.make_async_copy(wo_hbm, wo_ref, out_sem.at[0])
    out_copy.start()
    q_acc[...] = jnp.zeros_like(q_acc)
    kv_acc[...] = jnp.zeros_like(kv_acc)

    @pl.loop(0, steps)
    def _(step):
        for copy in fetch(step):
            copy.wait()
        cut = pl.ds(pl.multiple_of(step * chunk, chunk), chunk)
        x = jnp.concatenate([held_ref[:, cut], *(r[:, cut] for r in own_refs)], axis=0)
        wkv = jnp.concatenate(
            [kva_ref[0, :, cut], kvb_ref[0, :, cut], kva_ref[1, :, cut], kvb_ref[1, :, cut]],
            axis=0,
        )
        q_acc[...] += jnp.dot(x, wq_ref[cut, :], preferred_element_type=jnp.float32)
        kv_acc[...] += lax.dot_general(
            x, wkv, (((1,), (1,)), ((), ())), preferred_element_type=jnp.float32
        )

    core, xh, y, first_new = sc_ref[0], sc_ref[1], sc_ref[2], sc_ref[3]
    low = core == 0
    keys = kv_acc[:, :HD]
    values = kv_acc[:, HD:]
    keys = jnp.where(low, keys, pltpu.roll(keys, dh, axis=1)).astype(jnp.bfloat16)
    values = jnp.where(low, values, pltpu.roll(values, dh, axis=1)).astype(jnp.bfloat16)

    def place(shape, dim):
        i = lax.broadcasted_iota(jnp.int32, shape, dim)
        side = jnp.where(i < half, 1 - core, core)
        chip_x = ((i >> 6) & 1) ^ xh
        chip_y = ((i >> 4) & 3) ^ y
        return (chip_y * 4 + chip_x * 2 + side) * per + (i & (per - 1))

    row, col = place((rows, rows), 0), place((rows, rows), 1)
    visible = (col <= row) & ((col >= first_new) == (row >= first_new))
    scale = 1.0 / math.sqrt(HD)
    for h in range(q_acc.shape[1] // HD):
        head = slice(h * HD, (h + 1) * HD)
        q = q_acc[:, head].astype(jnp.bfloat16)
        scores = (
            lax.dot_general(q, keys, (((1,), (1,)), ((), ())), preferred_element_type=jnp.float32)
            * scale
        )
        scores = jnp.where(visible, scores, -1e30)
        top = jnp.max(scores, axis=1, keepdims=True)
        expo = jnp.where(visible, jnp.exp(scores - top), 0.0)
        weights = (expo / jnp.sum(expo, axis=1, keepdims=True)).astype(jnp.bfloat16)
        mixed = jnp.dot(weights, values, preferred_element_type=jnp.float32)
        o_ref[:, head] = mixed.astype(jnp.bfloat16)
    out_copy.wait()
    for cut in (slice(i, i + 512) for i in range(0, out_cols, 512)):
        y = jnp.dot(o_ref[...], wo_ref[:, cut], preferred_element_type=jnp.float32)
        other_ref[:, cut] = y[:half].astype(jnp.bfloat16)
        own_ref[:, cut] = y[half:].astype(jnp.bfloat16)


def attention(scalars, shards_in, wq, kv_mine, kv_other, wo, chunk=1024):
    per, depth = shards_in[0].shape
    n_shards = len(shards_in)
    rows = per * n_shards
    cols = wq.shape[1]
    dh = kv_mine.shape[1]
    part = jax.ShapeDtypeStruct((rows // 2, wo.shape[1]), jnp.bfloat16)
    return pl.pallas_call(
        functools.partial(attention_kernel, n_shards, chunk),
        out_shape=(part, part),
        in_specs=[SM] + [FAR] * (n_shards // 2) + [VM] * (n_shards // 2) + [FAR] * 4,
        out_specs=(VM,) * 2,
        scratch_shapes=[
            pltpu.VMEM((rows, cols), jnp.bfloat16),
            pltpu.VMEM((rows, cols), jnp.float32),
            pltpu.VMEM((rows, 4 * dh), jnp.float32),
            pltpu.VMEM(wq.shape, jnp.bfloat16),
            pltpu.VMEM(kv_mine.shape, jnp.bfloat16),
            pltpu.VMEM(kv_other.shape, jnp.bfloat16),
            pltpu.VMEM(wo.shape, jnp.bfloat16),
            pltpu.VMEM((rows // 2, depth), jnp.bfloat16),
            pltpu.SemaphoreType.DMA((3, depth // chunk)),
            pltpu.SemaphoreType.DMA((1,)),
            pltpu.SemaphoreType.DMA((n_shards // 2, depth // chunk)),
        ],
        compiler_params=kernel_params(32),
        cost_estimate=pl.CostEstimate(
            flops=2 * rows * depth * (cols + 4 * dh),
            bytes_accessed=2 * (rows * depth + depth * (cols + 4 * dh)),
            transcendentals=4 * rows * rows,
        ),
        name="attention",
    )(scalars, *map(far, shards_in[: n_shards // 2]), *shards_in[n_shards // 2 :], far(wq), far(kv_mine), far(kv_other), far(wo))


def add_kernel(n, *refs):
    outs = refs[2 * n :]
    per = outs[0].shape[0]
    width = refs[0].shape[1]
    for i, out in enumerate(outs):
        cut = slice(i * per, (i + 1) * per)
        for j in range(n):
            total = f32(refs[j][cut, :]) + f32(refs[n + j][cut, :])
            out[:, j * width : (j + 1) * width] = total.astype(jnp.bfloat16)


def add_pieces(kept, arrived, count):
    rows, cols = kept[0].shape
    out = jax.ShapeDtypeStruct((rows // count, cols * len(kept)), jnp.bfloat16)
    return pl.pallas_call(
        functools.partial(add_kernel, len(kept)),
        out_shape=(out,) * count,
        in_specs=[VM] * (2 * len(kept)),
        out_specs=(VM,) * count,
        compiler_params=kernel_params(4),
        name="add_pieces",
    )(*kept, *arrived)


def sum_kernel(*refs):
    total = f32(refs[0][...])
    for r in refs[1:-1]:
        total += f32(r[...])
    refs[-1][...] = total.astype(refs[-1].dtype)


def sum_of(arrays, dtype):
    return pl.pallas_call(
        sum_kernel,
        out_shape=jax.ShapeDtypeStruct(arrays[0].shape, dtype),
        in_specs=[VM] * len(arrays),
        out_specs=VM,
        compiler_params=kernel_params(4),
        name="sum_of",
    )(*arrays)


def slope_kernel(*refs):
    parts = refs[:-4]
    x_ref, sp_ref, next_ref, slope_ref = refs[-4:]
    blocks, rows, width = sp_ref.shape
    inner = jnp.zeros((rows, 1), jnp.float32)
    own_sq = jnp.zeros((rows, 1), jnp.float32)
    target_sq = jnp.zeros((rows, 1), jnp.float32)
    for j in range(blocks):
        cols = slice(j * width, (j + 1) * width)
        total = f32(parts[0][:, cols])
        for p in parts[1:]:
            total += f32(p[:, cols])
        new = (f32(x_ref[:, cols]) + total).astype(jnp.bfloat16)
        next_ref[:, cols] = new
        target = f32(new)
        sp = f32(sp_ref[j])
        inner += jnp.sum(sp * target, axis=1, keepdims=True)
        own_sq += jnp.sum(sp * sp, axis=1, keepdims=True)
        target_sq += jnp.sum(target * target, axis=1, keepdims=True)
    inv_own = lax.rsqrt(own_sq + COS_EPS)
    inv_target = lax.rsqrt(target_sq + COS_EPS)
    cosine = inner * inv_own * inv_target
    toward = inner * inv_target * inv_own * inv_own * inv_own
    away = inv_own * inv_target
    for j in range(blocks):
        cols = slice(j * width, (j + 1) * width)
        slope = LOSS_WEIGHT * (toward * f32(sp_ref[j]) - f32(next_ref[:, cols]) * away)
        slope_ref[j, :, :width] = slope.astype(jnp.bfloat16)
    distance = jnp.broadcast_to(1.0 - cosine, (rows, CARRY))
    high = f32(distance.astype(jnp.bfloat16))
    middle = f32((distance - high).astype(jnp.bfloat16))
    low = distance - high - middle
    lane = lax.broadcasted_iota(jnp.int32, (rows, CARRY), 1)
    carried = jnp.where(lane == 0, high, jnp.where(lane == 1, middle, low))
    carried = jnp.where(lane < 3, carried, 0.0).astype(jnp.bfloat16)
    for j in range(blocks):
        slope_ref[j, :, width:] = carried


def slopes(parts, x, sp):
    return pl.pallas_call(
        slope_kernel,
        out_shape=(
            jax.ShapeDtypeStruct(x.shape, jnp.bfloat16),
            jax.ShapeDtypeStruct((*sp.shape[:2], sp.shape[2] + CARRY), jnp.bfloat16),
        ),
        in_specs=[VM] * (len(parts) + 2),
        out_specs=(VM, VM),
        compiler_params=kernel_params(6),
        name="slopes",
    )(*parts, x, sp)


def stacked(refs, all_ref):
    for k, r in enumerate(refs):
        all_ref[:, k] = r[:, :, : all_ref.shape[3]]
    n_sec, n_y, rows, width = all_ref.shape
    return all_ref[...].reshape(n_sec * n_y * rows, width)


def blocks_of(sc_ref, size):
    core, xh = sc_ref[0], sc_ref[1]
    for at_x, at_c in ((xh, core), (xh, 1 - core), (1 - xh, core), (1 - xh, 1 - core)):
        yield pl.ds(pl.multiple_of((at_x * 2 + at_c) * size, size), size)


def student_proj_kernel(n_sends, sc_ref, *refs):
    distant, last_ref, keep_ref, send_refs = refs[:4], refs[4], refs[5], refs[6 : 6 + n_sends]
    near, sems = refs[6 + n_sends : -1], refs[-1]
    copies = fetched(distant, near, sems)
    tokens_ref, proj_refs = near[0], (*near[1:], last_ref)
    size = proj_refs[0].shape[0]
    total = None
    copies[0].wait()
    for cut, p, copy in zip(blocks_of(sc_ref, size), proj_refs, (*copies[1:], None)):
        if copy is not None:
            copy.wait()
        y = jnp.dot(tokens_ref[:, cut], p[...], preferred_element_type=jnp.float32)
        total = y if total is None else total + y
    n_sec, rows, block = keep_ref.shape
    total = total.reshape(n_sec, 1 + n_sends, rows, block)
    keep_ref[...] = total[:, 0]
    for k, out in enumerate(send_refs):
        out[...] = total[:, k + 1].astype(jnp.bfloat16)


def student_proj_part(scalars, tokens, proj, n_sec, n_y):
    n_tok, feats = tokens.shape
    rows, block = n_tok // (n_sec * n_y), proj[0].shape[1]
    keep = jax.ShapeDtypeStruct((n_sec, rows, block), jnp.float32)
    send = jax.ShapeDtypeStruct((n_sec, rows, block), jnp.bfloat16)
    inputs = (tokens, *proj[:3])
    return pl.pallas_call(
        functools.partial(student_proj_kernel, n_y - 1),
        out_shape=(keep,) + (send,) * (n_y - 1),
        in_specs=[SM] + [FAR] * len(inputs) + [VM],
        out_specs=(VM,) * n_y,
        scratch_shapes=[pltpu.VMEM(v.shape, v.dtype) for v in inputs]
        + [pltpu.SemaphoreType.DMA((len(inputs),))],
        compiler_params=kernel_params(14),
        cost_estimate=pl.CostEstimate(
            flops=2 * n_tok * feats * block,
            bytes_accessed=2 * (n_tok * feats + feats * block + n_tok * block),
            transcendentals=0,
        ),
        name="student_proj_part",
    )(scalars, *map(far, inputs), proj[3])


def turn_kernel(n, *refs):
    distant, outs, near, sems = refs[:n], refs[n : 2 * n], refs[2 * n : 3 * n], refs[-1]
    copies = fetched(distant, near, sems)
    for copy, v, out in zip(copies, near, outs):
        copy.wait()
        out[...] = v[...].T


def turned(values):
    return pl.pallas_call(
        functools.partial(turn_kernel, len(values)),
        out_shape=tuple(jax.ShapeDtypeStruct(v.shape[::-1], v.dtype) for v in values),
        in_specs=[FAR] * len(values),
        out_specs=(VM,) * len(values),
        scratch_shapes=[pltpu.VMEM(v.shape, v.dtype) for v in values]
        + [pltpu.SemaphoreType.DMA((len(values),))],
        compiler_params=kernel_params(14),
        name="turned",
    )(*map(far, values))


def gradients_kernel(n_y, sc_ref, *refs):
    slope_refs, tokens_ref, proj_refs = refs[:n_y], refs[n_y], refs[n_y + 1 : n_y + 5]
    loss_ref, away_far, away_near, stay_far, stay_near = refs[n_y + 5 : n_y + 10]
    piece_refs, all_ref, gs_ref = refs[n_y + 10 : -2], refs[-2], refs[-1]
    slope = stacked(slope_refs, all_ref)
    width, size = proj_refs[0].shape
    core, xh = sc_ref[0], sc_ref[1]
    for out, at_x, at_c in (
        (away_far, 1 - xh, 1 - core),
        (away_near, xh, 1 - core),
        (stay_far, 1 - xh, core),
        (stay_near, xh, core),
    ):
        cut = pl.ds(pl.multiple_of((at_x * 2 + at_c) * size, size), size)
        y = jnp.dot(tokens_ref[cut, :], slope, preferred_element_type=jnp.float32)
        out[...] = y.astype(out.dtype)
    for cut, p in zip(blocks_of(sc_ref, size), proj_refs):
        y = jnp.dot(slope, p[...], preferred_element_type=jnp.float32)
        n_z, n_xl, _, rows, _ = gs_ref.shape
        y = y.astype(jnp.bfloat16).reshape(n_z * n_xl, n_y, rows, size)
        for k in range(n_y):
            gs_ref[:, :, sc_ref[2] ^ k, :, cut] = y[:, k].reshape(n_z, n_xl, rows, size)
    for k, out in enumerate(piece_refs):
        out[...] = gs_ref[sc_ref[4] ^ k]
    loss = None
    for r in slope_refs:
        part = jnp.sum(f32(r[:, :, width:]), axis=(0, 1), keepdims=True)
        loss = part if loss is None else loss + part
    loss = jnp.sum(loss[0], axis=1, keepdims=True)
    loss_ref[...] = jnp.broadcast_to(loss, loss_ref.shape)


def gradients(scalars, slope, tokens_t, proj_t, n_z):
    n_y = len(slope)
    n_sec, rows = slope[0].shape[:2]
    width, size = proj_t[0].shape
    low = jax.ShapeDtypeStruct((size, width), jnp.bfloat16)
    high = jax.ShapeDtypeStruct((size, width), jnp.float32)
    shape = (n_z, n_sec // n_z, n_y, rows, size * len(proj_t))
    piece = jax.ShapeDtypeStruct(shape[1:], jnp.bfloat16)
    inputs = (tokens_t, *proj_t)
    return pl.pallas_call(
        functools.partial(gradients_kernel, n_y),
        out_shape=(
            jax.ShapeDtypeStruct((8, 128), jnp.float32),
            low,
            low,
            high,
            high,
            *(piece,) * n_z,
        ),
        in_specs=[SM] + [VM] * (n_y + len(inputs)),
        out_specs=(VM,) * (5 + n_z),
        scratch_shapes=[
            pltpu.VMEM((n_sec, n_y, rows, width), jnp.bfloat16),
            pltpu.VMEM(shape, jnp.bfloat16),
        ],
        compiler_params=kernel_params(12),
        name="gradients",
    )(scalars, *slope, *inputs)


def place_kernel(g_ref, o_ref):
    n_xl, n_y, _, feats = g_ref.shape
    for k in range(n_y):
        total = f32(g_ref[0, k])
        for s in range(1, n_xl):
            total += f32(g_ref[s, k])
        o_ref[:, k * feats : (k + 1) * feats] = total


def placed_feats(g):
    _, n_y, rows, feats = g.shape
    return pl.pallas_call(
        place_kernel,
        out_shape=jax.ShapeDtypeStruct((rows, feats * n_y), jnp.float32),
        in_specs=[VM],
        out_specs=VM,
        compiler_params=kernel_params(4),
        name="placed_feats",
    )(g)


def tied(*values):
    return lax.optimization_barrier(values)


def to_columns(value, n_y):
    return [value] + [swap(value, "y", k) for k in range(1, n_y)]


def step(
    teacher_rows,
    norm_gain,
    query_weight,
    keys_values,
    output_weight,
    doc_start,
    student_rows,
    projector,
):
    core = lax.axis_index("c").astype(jnp.int32)
    xh = lax.axis_index("xh").astype(jnp.int32)
    y = lax.axis_index("y").astype(jnp.int32)
    n_sec = lax.axis_size(SEC)
    n_y = lax.axis_size("y")
    n_tp = lax.axis_size(TP)
    x = teacher_rows[0]
    rows, _ = x.shape
    z = lax.axis_index("z").astype(jnp.int32)
    scalars = jnp.stack([core, xh, y, doc_start[0], z])

    feats = student_rows.shape[2] // n_y
    picked = [
        lax.dynamic_slice_in_dim(student_rows[0], (y ^ k) * feats, feats, axis=1)
        for k in range(n_y)
    ]
    picked = [picked[0]] + [swap(picked[k], "y", k) for k in range(1, n_y)]
    proj = [projector, swap(projector, "c", 1), swap(projector, "xh", 1)]

    normed = normalize(x, norm_gain)
    y1, y3 = swap(normed, "y", 1), swap(normed, "y", 3)
    across = swap(normed, "xh", 1)
    y2 = swap(normed, "y", 2)
    own = [normed, y1, y2, y3]
    own += [across, swap(across, "y", 1), swap(across, "y", 2), swap(across, "y", 3)]
    other = [swap(v, "c", 1) for v in own]
    kv_mine = jnp.swapaxes(keys_values[0], 1, 2)
    kv_other = swap(kv_mine, "c", 1)

    mine, _ = tied(jnp.stack(picked), normed)
    tokens = exchange(jnp.broadcast_to(mine, (n_sec, *mine.shape)), SEC)
    n_tok = n_sec * n_y * rows
    tokens = tokens.reshape(n_tok, feats)

    proj.append(swap(proj[2], "c", 1))
    to_other, kept = attention(
        scalars, other + own, query_weight[0], kv_mine, kv_other, output_weight[0]
    )
    arrived = swap(to_other, "c", 1)

    tokens, kept = tied(tokens, kept)
    keep, *sends = student_proj_part(scalars, tokens, proj, n_sec, n_y)
    got = [swap(sends[k - 1], "y", k) for k in range(1, n_y)]

    pieces = add_pieces([kept], [arrived], 2 * n_y)
    near, away = list(pieces[:n_y]), list(pieces[n_y:])
    relayed = swap(away[2], "xh", 1)
    away = sum_of((away[0], swap(away[1], "y", 1), swap(away[3], "y", 3)), jnp.bfloat16)
    away = swap(away, "xh", 1)
    relayed = swap(sum_of((near[2], relayed), jnp.bfloat16), "y", 2)
    parts = (near[0], swap(near[1], "y", 1), swap(near[3], "y", 3), relayed, away)

    sp = sum_of((keep, *got), jnp.bfloat16)
    sp = exchange(sp, SEC)
    teacher_next, slope = slopes(parts, x, sp)

    slope = exchange(slope, SEC)
    slope, tokens = tied(slope, tokens)
    slope = to_columns(slope, n_y)
    tokens_t, *proj_t = turned((tokens, *proj))
    loss, away_far, away_near, stay_far, stay_near, *grad_s = gradients(
        scalars, slope, tokens_t, proj_t, lax.axis_size("z")
    )
    for k in range(1, len(grad_s)):
        grad_s[k] = swap(grad_s[k], "z", k)
    loss = loss + swap(loss, "c", 1)
    away_far = swap(away_far, "c", 1)
    away_near = swap(away_near, "c", 1)
    loss = loss + swap(loss, "xh", 1)
    across = swap(sum_of((stay_far, away_far), jnp.bfloat16), "xh", 1)
    nearly = sum_of((stay_near, away_near), jnp.float32)
    loss = loss[:1, :1] / (n_sec * n_tp * rows)
    grad_s[2], nearly = tied(grad_s[2], nearly)
    grad_s = sum_of(grad_s, jnp.bfloat16)
    shape = grad_s.shape
    grad_s = exchange(grad_s.reshape(-1, *shape[2:]), ("xl", "y")).reshape(shape)
    grad_projector = sum_of((nearly, across), jnp.float32)
    grad_s, grad_projector = tied(grad_s, grad_projector)
    grad_student = placed_feats(grad_s)
    return (teacher_next[None], loss[0, 0], grad_student[None], grad_projector)


def solution(mesh):
    fine = Mesh(mesh.devices.reshape(4, 2, 4, 2, 2), ("z", "xl", "y", "xh", "c"))
    placed = (
        P(SEC, TP, None),
        P(SEC, None),
        P(SEC, None, TP),
        P(SEC, None, None, TP),
        P(SEC, TP, None),
        P(SEC),
        P(SEC, TP, None),
        P(TP, SEC),
    )
    return jax.shard_map(
        step,
        mesh=fine,
        in_specs=placed,
        out_specs=(P(SEC, TP, None), P(), P(SEC, TP, None), P(TP, SEC)),
        check_vma=False,
    )
```
